32 devices in a mesh: seq: 16 (over z, y, x), head: 2 (over core).
Axes of the slice: x: 2, y: 2, z: 4, core: 2. Of those that a mesh axis runs over, the one named last changes fastest.
Arguments:
- tokens: bfloat16 [2048, 1024], P('seq'), may hold values from -17 to 17
- w_query: bfloat16 [1024, 1024], P(None, 'head'), may hold values from -0.1875 to 0.1875
- w_key: bfloat16 [1024, 1024], P(None, 'head'), may hold values from -0.1875 to 0.1875
- w_value: bfloat16 [1024, 1024], P(None, 'head'), may hold values from -0.1875 to 0.1875
- w_out: bfloat16 [1024, 1024], P('head'), may hold values from -1.796875 to 1.796875
- cluster_ids: int32 [4, 2048], P('head', 'seq'), may hold values from 0 to 15, as said below
- positions: int32 [2048], P('seq'), may hold values from 0 to 2047, each once
Outputs:
- mixed: bfloat16 [2048, 1024], P(('seq', 'head'))
The draws below stay inside these ranges and needn't reach their ends.
Inputs may be any that keep to these rules, and one draw needn't show every extreme that they name: `cluster_ids`: in each head group every cluster holds at most 320 tokens, and at most 20 of the 128 tokens of one index of seq; both bounds are reached.
All inputs are finite; a program needn't handle non-finite values.
Results may differ from the reference program's by a relative error of at most 0.0029.
The reference program's roundings to bfloat16 on the way count: a program that leaves them out, or rounds other values in their place, can miss the bound.
Values may be sent and summed in bfloat16 or wider, within the bound.
No kernel may reach another device: no remote copies, remote signals or barrier semaphores. Data moves between devices by JAX's collectives and lax.ppermute only.
A program may use at most 64 MiB of HBM per device.

```python
import jax
import jax.numpy as jnp
from jax import lax

D = 1024
HEADS = 16
HD = 64
GROUPS = 4
TOK_DEV = 128
GROUP_HEADS = 4
TOKENS = 2048
NC = 16
CLUSTER_MAX = 320


def draw_tokens(key, part):
    base = jax.random.normal(jax.random.fold_in(key, 13), (TOKENS, D), jnp.float32)
    return jnp.clip(base, -6.0, 6.0).astype(jnp.bfloat16)


def one_group(group_key):
    half = TOK_DEV // 2
    fewer = NC // 4
    labels = jax.random.permutation(jax.random.fold_in(group_key, 1), NC).astype(jnp.int32)
    shift = jax.random.permutation(jax.random.fold_in(group_key, 2), NC).astype(jnp.int32)
    other = (jax.random.permutation(jax.random.fold_in(group_key, 3), NC) % fewer).astype(jnp.int32)
    slot = jnp.arange(half, dtype=jnp.int32)
    first = (slot[None, :] + shift[:, None]) % NC
    second = (slot[None, :] + other[:, None]) % fewer
    index = jnp.concatenate([labels[first], labels[second]], axis=1)
    scores = jax.random.randint(jax.random.fold_in(group_key, 4), (NC, TOK_DEV), 0, 2 ** 20) * TOK_DEV + jnp.arange(TOK_DEV, dtype=jnp.int32)[None, :]
    order = jnp.argsort(scores, axis=1)
    index = jnp.take_along_axis(index, order, axis=1)
    return index.reshape(TOKENS)


def draw_cluster_ids(key, part):
    keys = jax.random.split(jax.random.fold_in(key, 21), GROUPS)
    return jax.vmap(one_group)(keys).astype(jnp.int32)


def level_of(rng, dims, pieces, least, largest):
    def one(axis_at, parts):
        steps = jax.random.uniform(jax.random.fold_in(jax.random.fold_in(rng, 6), axis_at), (parts,), jnp.float32, least / len(pieces), largest / len(pieces))
        return jnp.repeat(jnp.exp(steps), dims[axis_at] // parts).reshape((-1,) + (1,) * (len(dims) - axis_at - 1))

    factor_of = one(*pieces[0])
    for cut in pieces[1:]:
        factor_of = factor_of * one(*cut)
    return factor_of


def noise(stream_key, dims, scale, limit, cuts=(), kind=jnp.bfloat16):
    drawn = jax.random.normal(stream_key, dims, jnp.float32) * scale
    if len(cuts) > 0:
        drawn = level_of(stream_key, dims, cuts, -0.22, 0.18) * drawn
    return jnp.clip(drawn, min=-limit, max=limit).astype(kind)


def setup_inputs(seed: int = 0) -> dict:
    key_list = jax.random.split(jax.random.key(seed), 8)
    return {
        "tokens": draw_tokens(jax.random.fold_in(key_list[7], 71), 0),
        "w_query": noise(key_list[1], (D, HEADS * HD), D ** -0.5, 0.1875, ((1, 2),)),
        "w_key": noise(key_list[2], (D, HEADS * HD), D ** -0.5, 0.1875, ((1, 2),)),
        "w_value": noise(key_list[3], (D, HEADS * HD), D ** -0.5, 0.1875, ((1, 2),)),
        "w_out": noise(key_list[4], (HEADS * HD, D), 0.3, 1.796875, ((0, 2),)),
        "cluster_ids": draw_cluster_ids(jax.random.fold_in(key_list[7], 71), 0),
        "positions": jax.random.permutation(key_list[6], TOKENS).astype(jnp.int32),
    }


def attend_rows(query, keys, values, query_pos, key_pos):
    scores = jnp.einsum("qhd,khd->hqk", query.astype(jnp.float32), keys.astype(jnp.float32)) * (HD ** -0.5)
    allowed = (key_pos[None, None, :] >= 0) & (key_pos[None, None, :] <= query_pos[None, :, None])
    masked = jnp.where(allowed, scores, jnp.float32(-1e30))
    top = jnp.max(masked, axis=-1, keepdims=True)
    expo = jnp.exp(masked - top)
    weights = (expo / jnp.sum(expo, axis=-1, keepdims=True)).astype(jnp.bfloat16)
    return jnp.einsum("hqk,khd->qhd", weights.astype(jnp.float32), values.astype(jnp.float32)).astype(jnp.bfloat16)


def reference(tokens, w_query, w_key, w_value, w_out, cluster_ids, positions):
    width = GROUP_HEADS * HD
    query = jnp.dot(tokens, w_query, preferred_element_type=jnp.float32).astype(jnp.bfloat16)
    keys = jnp.dot(tokens, w_key, preferred_element_type=jnp.float32).astype(jnp.bfloat16)
    values = jnp.dot(tokens, w_value, preferred_element_type=jnp.float32).astype(jnp.bfloat16)
    iota = jnp.arange(CLUSTER_MAX, dtype=jnp.int32)
    tok_index = jnp.arange(TOKENS, dtype=jnp.int32)
    results = []
    for group in range(GROUPS):
        ids = cluster_ids[group]
        order = jnp.argsort(ids * TOKENS + tok_index).astype(jnp.int32)
        counts = jax.ops.segment_sum(jnp.ones_like(ids), ids, num_segments=NC).astype(jnp.int32)
        starts = (jnp.cumsum(counts) - counts).astype(jnp.int32)
        padded = jnp.concatenate([order, jnp.zeros((CLUSTER_MAX,), jnp.int32)])
        lo = group * width
        q_group = query[:, lo:lo + width].reshape(TOKENS, GROUP_HEADS, HD)
        k_group = keys[:, lo:lo + width].reshape(TOKENS, GROUP_HEADS, HD)
        v_group = values[:, lo:lo + width].reshape(TOKENS, GROUP_HEADS, HD)

        def one_cluster(result, cluster):
            index = lax.dynamic_slice(padded, (starts[cluster].astype(jnp.int32),), (CLUSTER_MAX,))
            valid = iota < counts[cluster]
            pos = jnp.where(valid, positions[index], -1).astype(jnp.int32)
            out = attend_rows(q_group[index], k_group[index], v_group[index], pos, pos)
            target = jnp.where(valid, index, TOKENS).astype(jnp.int32)
            result = result.at[target].set(out.reshape(CLUSTER_MAX, width), mode="drop")
            return result, None

        result, _ = lax.scan(one_cluster, jnp.zeros((TOKENS, width), jnp.bfloat16), jnp.arange(NC, dtype=jnp.int32))
        results.append(result)
    attended = jnp.concatenate(results, axis=1)
    return jnp.dot(attended, w_out, preferred_element_type=jnp.float32).astype(jnp.bfloat16)
```

```python
import functools

import jax
import jax.numpy as jnp
from jax import lax
from jax.experimental import pallas as pl
from jax.experimental.pallas import tpu as pltpu
from jax.sharding import PartitionSpec as P

HD = 64
GROUP_HEADS = 4

SPLIT = 4
PLANE = 4
META = 16
BASE = 128
VMEM_LIMIT = 48 << 20
LOG2E = 1.4426950408889634


def project_kernel(tok_ref, pos_ref, cid_ref, wq_ref, wk_ref, wv_ref, *rest):
    kv0_ref, q0_ref, m1_ref, m2_ref, m3_ref, wbuf, qkv, sems = rest
    tok, cols = tok_ref.shape[0], wq_ref.shape[1]
    pair = cols // SPLIT
    half = cols // 2
    copies = []
    for part, w_ref in enumerate((wq_ref, wk_ref, wv_ref)):
        for side in range(2):
            lanes = pl.ds(side * half, half)
            copy = pltpu.make_async_copy(
                w_ref.at[:, lanes], wbuf.at[part, :, lanes], sems.at[part, side]
            )
            copy.start()
            copies.append((part, side, copy))
    rows = tok_ref[...]
    for part, side, copy in copies:
        copy.wait()
        result = jnp.dot(
            rows, wbuf[part, :, side * half : (side + 1) * half], preferred_element_type=jnp.float32
        )
        start = part * cols + side * half
        qkv[:, start : start + half] = result.astype(jnp.bfloat16)
    high_digit = jnp.broadcast_to(pos_ref[...] // BASE, (META, tok))
    low_digit = jnp.broadcast_to(pos_ref[...] % BASE, (META, tok))
    first = lax.broadcasted_iota(jnp.int32, (META, tok), 0) == 0
    chip = lax.axis_index("seq") // PLANE
    for step, refs in enumerate(((kv0_ref, q0_ref), (m1_ref,), (m2_ref,), (m3_ref,))):
        who = jnp.bitwise_xor(chip, step)
        kv_ref = refs[0]
        lo = pl.multiple_of(who * pair, pair)
        query = qkv[:, pl.ds(lo, pair)]
        kv_ref[:tok, :pair] = qkv[:, pl.ds(pl.multiple_of(cols + lo, pair), pair)]
        kv_ref[:tok, pair:] = qkv[:, pl.ds(pl.multiple_of(2 * cols + lo, pair), pair)]
        ids = jnp.where(who >= SPLIT // 2, cid_ref[1:2, :], cid_ref[0:1, :])
        left = jnp.where(first, jnp.broadcast_to(ids, (META, tok)), low_digit)
        kv_ref[tok : tok + META, :pair] = left.astype(jnp.float32).astype(jnp.bfloat16)
        kv_ref[tok : tok + META, pair:] = high_digit.astype(jnp.float32).astype(jnp.bfloat16)
        q_ref, base = (refs[1], 0) if step == 0 else (kv_ref, tok + META)
        q_ref[base : base + tok // 2, :pair] = query[: tok // 2]
        q_ref[base : base + tok // 2, pair:] = query[tok // 2 :]


def project(tokens, positions, cluster_ids, w_query, w_key, w_value):
    tok, depth = tokens.shape
    cols = w_query.shape[1]
    wide = 2 * cols // SPLIT
    vmem = pl.BlockSpec(memory_space=pltpu.VMEM)
    hbm = pl.BlockSpec(memory_space=pl.ANY)
    full = tok + META + tok // 2

    def shape(rows):
        return jax.ShapeDtypeStruct((rows, wide), jnp.bfloat16)

    return pl.pallas_call(
        project_kernel,
        out_shape=(shape(tok + META), shape(tok // 2), shape(full), shape(full), shape(full)),
        in_specs=[vmem, vmem, vmem, hbm, hbm, hbm],
        out_specs=(vmem,) * 5,
        scratch_shapes=[
            pltpu.VMEM((3, depth, cols), jnp.bfloat16),
            pltpu.VMEM((tok, 3 * cols), jnp.bfloat16),
            pltpu.SemaphoreType.DMA((3, 2)),
        ],
        compiler_params=pltpu.CompilerParams(vmem_limit_bytes=VMEM_LIMIT),
        cost_estimate=pl.CostEstimate(
            flops=6 * tok * depth * cols, bytes_accessed=6 * depth * cols, transcendentals=0
        ),
        name="project",
    )(tokens, positions.reshape(1, tok), cluster_ids, w_query, w_key, w_value)


def attend_kernel(total, tok, *refs):
    q_refs = refs[:SPLIT]
    kv_refs = refs[SPLIT : SPLIT + 2 * PLANE]
    out_refs = refs[SPLIT + 2 * PLANE : SPLIT + 2 * PLANE + SPLIT]
    keys, values, codes, column = refs[SPLIT + 2 * PLANE + SPLIT :]
    pair = keys.shape[1]
    block = tok + META
    stride = 2 * total

    def ids_of(ref, base):
        cid = ref[base + tok : base + tok + 1, :pair].astype(jnp.float32)
        low = ref[base + tok + 1 : base + tok + 2, :pair].astype(jnp.float32)
        high = ref[base + tok : base + tok + 1, pair:].astype(jnp.float32)
        pos = high * float(BASE) + low
        return cid * float(stride) + pos, pos

    at = 0
    for ref in kv_refs:
        for item in range(ref.shape[0] // block):
            base = item * block
            keys[at : at + tok, :] = ref[base : base + tok, :pair]
            values[at : at + tok, :] = ref[base : base + tok, pair:]
            codes[0:1, at : at + tok] = ids_of(ref, base)[0]
            at += tok
    lane = lax.broadcasted_iota(jnp.int32, (tok, pair), 1) < HD
    key_codes = codes[0:1, :]
    scale = HD**-0.5 * LOG2E
    for item in range(SPLIT):
        ref, base = (kv_refs[0], 0) if item == 0 else (kv_refs[1], (item - 1) * block)
        code, pos = ids_of(ref, base)
        column[0:1, :] = code
        column[1:2, :] = pos
        turned = jnp.transpose(column[...])
        gap = turned[:, 0:1] - key_codes
        allowed = (gap >= 0.0) & (gap <= turned[:, 1:2])
        bias = jnp.where(allowed, 0.0, -1e30)
        q_ref = q_refs[item]
        start = q_ref.shape[0] - tok // 2
        query = jnp.concatenate([q_ref[start:, :pair], q_ref[start:, pair:]], axis=0)
        results = []
        for head in range(2):
            own = jnp.where(lane if head == 0 else jnp.logical_not(lane), query, jnp.zeros_like(query))
            scores = lax.dot_general(
                own, keys[...], (((1,), (1,)), ((), ())), preferred_element_type=jnp.float32
            )
            scores = scores * scale + bias
            top = jnp.max(scores, axis=1, keepdims=True)
            expo = jnp.exp2(scores - top)
            weights = expo * (1.0 / jnp.sum(expo, axis=1, keepdims=True))
            results.append(
                jnp.dot(weights.astype(jnp.bfloat16), values[...], preferred_element_type=jnp.float32)
            )
        out_refs[item][...] = jnp.where(lane, results[0], results[1]).astype(jnp.bfloat16)


def attend(total, tok, queries, sources):
    pair = sources[0].shape[1] // 2
    vmem = pl.BlockSpec(memory_space=pltpu.VMEM)
    count = SPLIT * PLANE * tok
    return pl.pallas_call(
        functools.partial(attend_kernel, total, tok),
        out_shape=(jax.ShapeDtypeStruct((tok, pair), jnp.bfloat16),) * SPLIT,
        in_specs=[vmem] * (len(queries) + len(sources)),
        out_specs=(vmem,) * SPLIT,
        scratch_shapes=[
            pltpu.VMEM((count, pair), jnp.bfloat16),
            pltpu.VMEM((count, pair), jnp.bfloat16),
            pltpu.VMEM((8, count), jnp.float32),
            pltpu.VMEM((8, tok), jnp.float32),
        ],
        compiler_params=pltpu.CompilerParams(vmem_limit_bytes=VMEM_LIMIT),
        cost_estimate=pl.CostEstimate(
            flops=8 * SPLIT * tok * count * pair,
            bytes_accessed=4 * count * pair,
            transcendentals=2 * SPLIT * tok * count,
        ),
        name="attend",
    )(*queries, *sources)


def mix_kernel(*refs):
    own_refs, other_refs = refs[:SPLIT], refs[SPLIT : 2 * SPLIT]
    w_own, w_other, out_ref, left, right = refs[2 * SPLIT :]
    rows, pair = out_ref.shape[0], own_refs[0].shape[1]
    chip = lax.axis_index("seq") // PLANE
    mine = pl.ds(pl.multiple_of(lax.axis_index("head") * rows, rows), rows)
    for step in range(SPLIT):
        lanes = pl.ds(pl.multiple_of(jnp.bitwise_xor(chip, step) * pair, pair), pair)
        left[:, lanes] = own_refs[step][mine, :]
        right[:, lanes] = other_refs[step][mine, :]
    total = jnp.dot(left[...], w_own[...], preferred_element_type=jnp.float32)
    total += jnp.dot(right[...], w_other[...], preferred_element_type=jnp.float32)
    out_ref[...] = total.astype(jnp.bfloat16)


def mix(own, other, w_own, w_other):
    rows = own[0].shape[0] // 2
    deep, width = w_own.shape
    vmem = pl.BlockSpec(memory_space=pltpu.VMEM)
    return pl.pallas_call(
        mix_kernel,
        out_shape=jax.ShapeDtypeStruct((rows, width), jnp.bfloat16),
        in_specs=[vmem] * (2 * SPLIT + 2),
        out_specs=vmem,
        scratch_shapes=[pltpu.VMEM((rows, deep), jnp.bfloat16)] * 2,
        compiler_params=pltpu.CompilerParams(vmem_limit_bytes=VMEM_LIMIT),
        cost_estimate=pl.CostEstimate(
            flops=4 * rows * deep * width, bytes_accessed=4 * deep * width, transcendentals=0
        ),
        name="mix",
    )(*own, *other, w_own, w_other)


def per_device_split(tokens, w_query, w_key, w_value, w_out, cluster_ids, positions):
    tok = tokens.shape[0]
    owners = lax.axis_size("seq")
    block = tok + META

    def send(array, bits):
        return lax.ppermute(array, "seq", [(i, i ^ bits) for i in range(owners)])

    def swap(array):
        return lax.ppermute(array, "head", [(0, 1), (1, 0)])

    w_other = swap(w_out)
    kv0, q0, m1, m2, m3 = project(tokens, positions, cluster_ids, w_query, w_key, w_value)
    r2 = send(m2, 2 * PLANE)
    r3 = send(m3, 3 * PLANE)
    r1 = send(m1, PLANE)
    rest = jnp.concatenate([r1[:block], r2[:block], r3[:block]], axis=0)
    sources = [kv0, rest]
    for bits in (1, 2, 3):
        sources += [send(kv0, bits), send(rest, bits)]
    a0, a1, a2, a3 = attend(owners * tok, tok, (q0, r1, r2, r3), sources)
    b2 = send(a2, 2 * PLANE)
    b3 = send(a3, 3 * PLANE)
    b1 = send(a1, PLANE)
    own = (a0, b1, b2, b3)
    return mix(own, tuple(swap(item) for item in own), w_out, w_other)


def attend_rows(query, keys, values, query_pos, key_pos):
    scores = jnp.einsum("qhd,khd->hqk", query, keys, preferred_element_type=jnp.float32) * HD ** (
        -0.5
    )
    allowed = (key_pos[None, None, :] >= 0) & (key_pos[None, None, :] <= query_pos[None, :, None])
    masked = jnp.where(allowed, scores, jnp.float32(-1e30))
    top = jnp.max(masked, axis=-1, keepdims=True)
    expo = jnp.exp(masked - top)
    weights = (expo / jnp.sum(expo, axis=-1, keepdims=True)).astype(jnp.bfloat16)
    return jnp.einsum("hqk,khd->qhd", weights, values, preferred_element_type=jnp.float32).astype(
        jnp.bfloat16
    )


def attend_group(data, pos):
    rows = data.shape[0]
    width = data.shape[1] // 3
    query = data[:, :width].reshape(rows, GROUP_HEADS, HD)
    keys = data[:, width : 2 * width].reshape(rows, GROUP_HEADS, HD)
    values = data[:, 2 * width :].reshape(rows, GROUP_HEADS, HD)
    half = rows // 2
    first = attend_rows(query[:half], keys, values, pos[:half], pos)
    second = attend_rows(query[half:], keys, values, pos[half:], pos)
    result = jnp.concatenate([first, second], axis=0)
    return result.reshape(rows, width)


def owner_side(pieces):
    data, pos = pieces
    outputs = [attend_group(data[:, item], pos[:, item]) for item in range(data.shape[1])]
    result = jnp.stack(outputs, axis=1)
    return lax.all_to_all(result, "seq", split_axis=0, concat_axis=0, tiled=True)


def per_device_owner(tokens, w_query, w_key, w_value, w_out, cluster_ids, positions):
    tok = tokens.shape[0]
    groups_here = cluster_ids.shape[0]
    owners = lax.axis_size("seq")
    half = tok // 2
    fewer = owners // 4
    capacity = (half + owners - 1) // owners + (half + fewer - 1) // fewer
    slots = owners * capacity
    width = w_query.shape[1] // groups_here
    tok_ids = jnp.arange(tok, dtype=jnp.int32)
    earlier = tok_ids[None, :] < tok_ids[:, None]
    same = cluster_ids[:, :, None] == cluster_ids[:, None, :]
    rank = jnp.sum((same & earlier[None]).astype(jnp.int32), axis=2)
    dest = cluster_ids * capacity + rank
    slot_ids = jnp.arange(slots, dtype=jnp.int32)
    matches = slot_ids[None, :, None] == dest[:, None, :]
    onehot = matches.astype(jnp.bfloat16)
    filled = jnp.any(matches, axis=2)
    pos_sum = jnp.sum(jnp.where(matches, positions[None, None, :], 0), axis=2)
    pos_slots = jnp.where(filled, pos_sum, -1).T

    def project_group(index):
        lo = index * width
        parts = [
            jnp.dot(tokens, weight[:, lo : lo + width], preferred_element_type=jnp.float32).astype(
                jnp.bfloat16
            )
            for weight in (w_query, w_key, w_value)
        ]
        return jnp.concatenate(parts, axis=1)

    data = jnp.stack([project_group(index) for index in range(groups_here)], axis=1)
    send = jnp.einsum("gst,tgc->sgc", onehot, data, preferred_element_type=jnp.float32).astype(
        jnp.bfloat16
    )
    back = owner_side(
        (
            lax.all_to_all(send, "seq", split_axis=0, concat_axis=0, tiled=True),
            lax.all_to_all(pos_slots, "seq", split_axis=0, concat_axis=0, tiled=True),
        )
    )
    attended = jnp.einsum("gst,sgc->tgc", onehot, back, preferred_element_type=jnp.float32).astype(
        jnp.bfloat16
    )
    attended = attended.reshape(tok, groups_here * width)
    mixed = lax.psum_scatter(
        jnp.dot(attended, w_out, preferred_element_type=jnp.float32),
        "head",
        scatter_dimension=0,
        tiled=True,
    )
    return mixed.astype(jnp.bfloat16)


def solution(mesh):
    in_specs = (
        P("seq", None),
        P(None, "head"),
        P(None, "head"),
        P(None, "head"),
        P("head", None),
        P("head", "seq"),
        P("seq"),
    )
    out_specs = P(("seq", "head"), None)
    plan = per_device_split if mesh.shape["seq"] == SPLIT * PLANE else per_device_owner
    return jax.shard_map(
        plan, mesh=mesh, in_specs=in_specs, out_specs=out_specs, check_vma=False
    )
```

```python
import functools

import jax
import jax.numpy as jnp
from jax import lax
from jax.experimental import pallas as pl
from jax.experimental.pallas import tpu as pltpu
from jax.sharding import PartitionSpec as P

HD = 64
GROUP_HEADS = 4

SPLIT = 4
PLANE = 4
META = 16
BASE = 128
VMEM_LIMIT = 48 << 20
PACK_LIMIT = 4 << 20
LOG2E = 1.4426950408889634


def project_kernel(tok_ref, pos_ref, cid_ref, wq_ref, wk_ref, wv_ref, *rest):
    kv0_ref, q0_ref, m1_ref, m2_ref, m3_ref, rows, wbuf, qkv, sems, rows_sem = rest
    tok, cols = tok_ref.shape[0], wq_ref.shape[1]
    pair = cols // SPLIT
    half = cols // 2
    rows_copy = pltpu.make_async_copy(tok_ref, rows, rows_sem)
    rows_copy.start()
    copies = []
    for part, w_ref in enumerate((wq_ref, wk_ref, wv_ref)):
        for side in range(2):
            lanes = pl.ds(side * half, half)
            copy = pltpu.make_async_copy(
                w_ref.at[:, lanes], wbuf.at[part, :, lanes], sems.at[part, side]
            )
            copy.start()
            copies.append((part, side, copy))
    rows_copy.wait()
    for part, side, copy in copies:
        copy.wait()
        result = jnp.dot(
            rows[...],
            wbuf[part, :, side * half : (side + 1) * half],
            preferred_element_type=jnp.float32,
        )
        start = part * cols + side * half
        qkv[:, start : start + half] = result.astype(jnp.bfloat16)
    high_digit = jnp.broadcast_to(pos_ref[...] // BASE, (META, tok))
    low_digit = jnp.broadcast_to(pos_ref[...] % BASE, (META, tok))
    first = lax.broadcasted_iota(jnp.int32, (META, tok), 0) == 0
    chip = lax.axis_index("seq") // PLANE
    for step, refs in enumerate(((kv0_ref, q0_ref), (m1_ref,), (m2_ref,), (m3_ref,))):
        who = jnp.bitwise_xor(chip, step)
        kv_ref = refs[0]
        lo = pl.multiple_of(who * pair, pair)
        query = qkv[:, pl.ds(lo, pair)]
        kv_ref[:tok, :pair] = qkv[:, pl.ds(pl.multiple_of(cols + lo, pair), pair)]
        kv_ref[:tok, pair:] = qkv[:, pl.ds(pl.multiple_of(2 * cols + lo, pair), pair)]
        ids = jnp.where(who >= SPLIT // 2, cid_ref[1:2, :], cid_ref[0:1, :])
        left = jnp.where(first, jnp.broadcast_to(ids, (META, tok)), low_digit)
        kv_ref[tok : tok + META, :pair] = left.astype(jnp.float32).astype(jnp.bfloat16)
        kv_ref[tok : tok + META, pair:] = high_digit.astype(jnp.float32).astype(jnp.bfloat16)
        q_ref, base = (refs[1], 0) if step == 0 else (kv_ref, tok + META)
        q_ref[base : base + tok // 2, :pair] = query[: tok // 2]
        q_ref[base : base + tok // 2, pair:] = query[tok // 2 :]


def project(tokens, positions, cluster_ids, w_query, w_key, w_value):
    tok, depth = tokens.shape
    cols = w_query.shape[1]
    wide = 2 * cols // SPLIT
    vmem = pl.BlockSpec(memory_space=pltpu.VMEM)
    hbm = pl.BlockSpec(memory_space=pltpu.HBM)
    full = tok + META + tok // 2

    def shape(rows):
        return jax.ShapeDtypeStruct((rows, wide), jnp.bfloat16)

    return pl.pallas_call(
        project_kernel,
        out_shape=(shape(tok + META), shape(tok // 2), shape(full), shape(full), shape(full)),
        in_specs=[hbm, vmem, vmem, hbm, hbm, hbm],
        out_specs=(vmem,) * 5,
        scratch_shapes=[
            pltpu.VMEM((tok, depth), jnp.bfloat16),
            pltpu.VMEM((3, depth, cols), jnp.bfloat16),
            pltpu.VMEM((tok, 3 * cols), jnp.bfloat16),
            pltpu.SemaphoreType.DMA((3, 2)),
            pltpu.SemaphoreType.DMA(()),
        ],
        cost_estimate=pl.CostEstimate(
            flops=6 * tok * depth * cols, bytes_accessed=6 * depth * cols, transcendentals=0
        ),
        name="project",
    )(tokens, positions.reshape(1, tok), cluster_ids, w_query, w_key, w_value)


def pack_kernel(first_ref, second_ref, out_ref):
    half = out_ref.shape[0] // 2
    out_ref[:half, :] = first_ref[:half, :]
    out_ref[half:, :] = second_ref[:half, :]


def pack(first, second, block, flops):
    vmem = pl.BlockSpec(memory_space=pltpu.VMEM)
    wide = first.shape[1]
    return pl.pallas_call(
        pack_kernel,
        out_shape=jax.ShapeDtypeStruct((2 * block, wide), jnp.bfloat16),
        in_specs=[vmem, vmem],
        out_specs=vmem,
        compiler_params=pltpu.CompilerParams(vmem_limit_bytes=PACK_LIMIT),
        cost_estimate=pl.CostEstimate(
            flops=flops, bytes_accessed=8 * block * wide, transcendentals=0
        ),
        name="pack",
    )(first, second)


def attend_kernel(total, tok, *refs):
    q_refs = refs[:SPLIT]
    kv_refs = refs[SPLIT : SPLIT + 2 * PLANE]
    out_refs = refs[SPLIT + 2 * PLANE : SPLIT + 2 * PLANE + SPLIT]
    keys, values, codes, column = refs[SPLIT + 2 * PLANE + SPLIT :]
    pair = keys.shape[1]
    block = tok + META
    stride = 2 * total

    def ids_of(ref, base):
        cid = ref[base + tok : base + tok + 1, :pair].astype(jnp.float32)
        low = ref[base + tok + 1 : base + tok + 2, :pair].astype(jnp.float32)
        high = ref[base + tok : base + tok + 1, pair:].astype(jnp.float32)
        pos = high * float(BASE) + low
        return cid * float(stride) + pos, pos

    at = 0
    for ref in kv_refs:
        for item in range(ref.shape[0] // block):
            base = item * block
            keys[at : at + tok, :] = ref[base : base + tok, :pair]
            values[at : at + tok, :] = ref[base : base + tok, pair:]
            codes[0:1, at : at + tok] = ids_of(ref, base)[0]
            at += tok
    lane = lax.broadcasted_iota(jnp.int32, (tok, pair), 1) < HD
    key_codes = codes[0:1, :]
    scale = HD**-0.5 * LOG2E
    for item in range(SPLIT):
        ref, base = kv_refs[item // 2], (item % 2) * block
        code, pos = ids_of(ref, base)
        column[0:1, :] = code
        column[1:2, :] = pos
        turned = jnp.transpose(column[...])
        gap = turned[:, 0:1] - key_codes
        allowed = (gap >= 0.0) & (gap <= turned[:, 1:2])
        bias = jnp.where(allowed, 0.0, -1e30)
        q_ref = q_refs[item]
        start = q_ref.shape[0] - tok // 2
        query = jnp.concatenate([q_ref[start:, :pair], q_ref[start:, pair:]], axis=0)
        results = []
        for head in range(2):
            own = jnp.where(lane if head == 0 else jnp.logical_not(lane), query, jnp.zeros_like(query))
            scores = lax.dot_general(
                own, keys[...], (((1,), (1,)), ((), ())), preferred_element_type=jnp.float32
            )
            scores = scores * scale + bias
            top = jnp.max(scores, axis=1, keepdims=True)
            expo = jnp.exp2(scores - top)
            weights = expo * (1.0 / jnp.sum(expo, axis=1, keepdims=True))
            results.append(
                jnp.dot(weights.astype(jnp.bfloat16), values[...], preferred_element_type=jnp.float32)
            )
        out_refs[item][...] = jnp.where(lane, results[0], results[1]).astype(jnp.bfloat16)


def attend(total, tok, queries, sources):
    pair = sources[0].shape[1] // 2
    vmem = pl.BlockSpec(memory_space=pltpu.VMEM)
    count = SPLIT * PLANE * tok
    return pl.pallas_call(
        functools.partial(attend_kernel, total, tok),
        out_shape=(jax.ShapeDtypeStruct((tok, pair), jnp.bfloat16),) * SPLIT,
        in_specs=[vmem] * (len(queries) + len(sources)),
        out_specs=(vmem,) * SPLIT,
        scratch_shapes=[
            pltpu.VMEM((count, pair), jnp.bfloat16),
            pltpu.VMEM((count, pair), jnp.bfloat16),
            pltpu.VMEM((8, count), jnp.float32),
            pltpu.VMEM((8, tok), jnp.float32),
        ],
        compiler_params=pltpu.CompilerParams(vmem_limit_bytes=VMEM_LIMIT),
        cost_estimate=pl.CostEstimate(
            flops=8 * SPLIT * tok * count * pair,
            bytes_accessed=4 * count * pair,
            transcendentals=2 * SPLIT * tok * count,
        ),
        name="attend",
    )(*queries, *sources)


def mix_kernel(*refs):
    own_refs, other_refs = refs[:SPLIT], refs[SPLIT : 2 * SPLIT]
    w_own, w_other, out_ref, left, right = refs[2 * SPLIT :]
    rows, pair = out_ref.shape[0], own_refs[0].shape[1]
    chip = lax.axis_index("seq") // PLANE
    mine = pl.ds(pl.multiple_of(lax.axis_index("head") * rows, rows), rows)
    for step in range(SPLIT):
        lanes = pl.ds(pl.multiple_of(jnp.bitwise_xor(chip, step) * pair, pair), pair)
        left[:, lanes] = own_refs[step][mine, :]
        right[:, lanes] = other_refs[step][mine, :]
    total = jnp.dot(left[...], w_own[...], preferred_element_type=jnp.float32)
    total += jnp.dot(right[...], w_other[...], preferred_element_type=jnp.float32)
    out_ref[...] = total.astype(jnp.bfloat16)


def mix(own, other, w_own, w_other):
    rows = own[0].shape[0] // 2
    deep, width = w_own.shape
    vmem = pl.BlockSpec(memory_space=pltpu.VMEM)
    return pl.pallas_call(
        mix_kernel,
        out_shape=jax.ShapeDtypeStruct((rows, width), jnp.bfloat16),
        in_specs=[vmem] * (2 * SPLIT + 2),
        out_specs=vmem,
        scratch_shapes=[pltpu.VMEM((rows, deep), jnp.bfloat16)] * 2,
        compiler_params=pltpu.CompilerParams(vmem_limit_bytes=VMEM_LIMIT),
        cost_estimate=pl.CostEstimate(
            flops=4 * rows * deep * width, bytes_accessed=4 * deep * width, transcendentals=0
        ),
        name="mix",
    )(*own, *other, w_own, w_other)


def per_device_split(tokens, w_query, w_key, w_value, w_out, cluster_ids, positions):
    tok = tokens.shape[0]
    owners = lax.axis_size("seq")
    block = tok + META

    def send(array, bits):
        return lax.ppermute(array, "seq", [(i, i ^ bits) for i in range(owners)])

    def swap(array):
        return lax.ppermute(array, "head", [(0, 1), (1, 0)])

    w_other = swap(w_out)
    kv0, q0, m1, m2, m3 = project(tokens, positions, cluster_ids, w_query, w_key, w_value)
    r1 = send(m1, PLANE)
    r2 = send(m2, 2 * PLANE)
    r3 = send(m3, 3 * PLANE)
    kv0, w_other = lax.optimization_barrier((kv0, w_other))
    near = pack(kv0, r1, block, 0)
    nears = [send(near, bits) for bits in (1, 2, 3)]
    far = pack(r2, r3, block, 10**10)
    far, *nears = lax.optimization_barrier((far, *nears))
    fars = [send(far, bits) for bits in (1, 2, 3)]
    sources = [near, far, *nears, *fars]
    a0, a1, a2, a3 = attend(owners * tok, tok, (q0, r1, r2, r3), sources)
    b2 = send(a2, 2 * PLANE)
    b3 = send(a3, 3 * PLANE)
    b1 = send(a1, PLANE)
    own = (a0, b1, b2, b3)
    return mix(own, tuple(swap(item) for item in own), w_out, w_other)


def attend_rows(query, keys, values, query_pos, key_pos):
    scores = jnp.einsum("qhd,khd->hqk", query, keys, preferred_element_type=jnp.float32) * HD ** (
        -0.5
    )
    allowed = (key_pos[None, None, :] >= 0) & (key_pos[None, None, :] <= query_pos[None, :, None])
    masked = jnp.where(allowed, scores, jnp.float32(-1e30))
    top = jnp.max(masked, axis=-1, keepdims=True)
    expo = jnp.exp(masked - top)
    weights = (expo / jnp.sum(expo, axis=-1, keepdims=True)).astype(jnp.bfloat16)
    return jnp.einsum("hqk,khd->qhd", weights, values, preferred_element_type=jnp.float32).astype(
        jnp.bfloat16
    )


def attend_group(data, pos):
    rows = data.shape[0]
    width = data.shape[1] // 3
    query = data[:, :width].reshape(rows, GROUP_HEADS, HD)
    keys = data[:, width : 2 * width].reshape(rows, GROUP_HEADS, HD)
    values = data[:, 2 * width :].reshape(rows, GROUP_HEADS, HD)
    half = rows // 2
    first = attend_rows(query[:half], keys, values, pos[:half], pos)
    second = attend_rows(query[half:], keys, values, pos[half:], pos)
    result = jnp.concatenate([first, second], axis=0)
    return result.reshape(rows, width)


def owner_side(pieces):
    data, pos = pieces
    outputs = [attend_group(data[:, item], pos[:, item]) for item in range(data.shape[1])]
    result = jnp.stack(outputs, axis=1)
    return lax.all_to_all(result, "seq", split_axis=0, concat_axis=0, tiled=True)


def per_device_owner(tokens, w_query, w_key, w_value, w_out, cluster_ids, positions):
    tok = tokens.shape[0]
    groups_here = cluster_ids.shape[0]
    owners = lax.axis_size("seq")
    half = tok // 2
    fewer = owners // 4
    capacity = (half + owners - 1) // owners + (half + fewer - 1) // fewer
    slots = owners * capacity
    width = w_query.shape[1] // groups_here
    tok_ids = jnp.arange(tok, dtype=jnp.int32)
    earlier = tok_ids[None, :] < tok_ids[:, None]
    same = cluster_ids[:, :, None] == cluster_ids[:, None, :]
    rank = jnp.sum((same & earlier[None]).astype(jnp.int32), axis=2)
    dest = cluster_ids * capacity + rank
    slot_ids = jnp.arange(slots, dtype=jnp.int32)
    matches = slot_ids[None, :, None] == dest[:, None, :]
    onehot = matches.astype(jnp.bfloat16)
    filled = jnp.any(matches, axis=2)
    pos_sum = jnp.sum(jnp.where(matches, positions[None, None, :], 0), axis=2)
    pos_slots = jnp.where(filled, pos_sum, -1).T

    def project_group(index):
        lo = index * width
        parts = [
            jnp.dot(tokens, weight[:, lo : lo + width], preferred_element_type=jnp.float32).astype(
                jnp.bfloat16
            )
            for weight in (w_query, w_key, w_value)
        ]
        return jnp.concatenate(parts, axis=1)

    data = jnp.stack([project_group(index) for index in range(groups_here)], axis=1)
    send = jnp.einsum("gst,tgc->sgc", onehot, data, preferred_element_type=jnp.float32).astype(
        jnp.bfloat16
    )
    back = owner_side(
        (
            lax.all_to_all(send, "seq", split_axis=0, concat_axis=0, tiled=True),
            lax.all_to_all(pos_slots, "seq", split_axis=0, concat_axis=0, tiled=True),
        )
    )
    attended = jnp.einsum("gst,sgc->tgc", onehot, back, preferred_element_type=jnp.float32).astype(
        jnp.bfloat16
    )
    attended = attended.reshape(tok, groups_here * width)
    mixed = lax.psum_scatter(
        jnp.dot(attended, w_out, preferred_element_type=jnp.float32),
        "head",
        scatter_dimension=0,
        tiled=True,
    )
    return mixed.astype(jnp.bfloat16)


def solution(mesh):
    in_specs = (
        P("seq", None),
        P(None, "head"),
        P(None, "head"),
        P(None, "head"),
        P("head", None),
        P("head", "seq"),
        P("seq"),
    )
    out_specs = P(("seq", "head"), None)
    plan = per_device_split if mesh.shape["seq"] == SPLIT * PLANE else per_device_owner
    return jax.shard_map(
        plan, mesh=mesh, in_specs=in_specs, out_specs=out_specs, check_vma=False
    )
```

```python
import functools

import jax
import jax.numpy as jnp
from jax import lax
from jax.experimental import pallas as pl
from jax.experimental.pallas import tpu as pltpu
from jax.sharding import PartitionSpec as P

HD = 64
GROUP_HEADS = 4

SPLIT = 4
PLANE = 4
META = 16
BASE = 128
PACK_LIMIT = 4 << 20
ATTEND_LIMIT = 16 << 20
EARLY_FLOPS = 8 * 10**9
LATE_FLOPS = (3 * 10**9,) * SPLIT
LOG2E = 1.4426950408889634


def project_kernel(tok_ref, pos_ref, cid_ref, wq_ref, wk_ref, wv_ref, *rest):
    kv0_ref, q0_ref, m1_ref, m2_ref, m3_ref, rows, wbuf, qkv, sems, rows_sem = rest
    tok, cols = tok_ref.shape[0], wq_ref.shape[1]
    pair = cols // SPLIT
    rows_copy = pltpu.make_async_copy(tok_ref, rows, rows_sem)
    rows_copy.start()
    copies = []
    for part, w_ref in enumerate((wq_ref, wk_ref, wv_ref)):
        copy = pltpu.make_async_copy(w_ref, wbuf.at[part], sems.at[part])
        copy.start()
        copies.append(copy)
    rows_copy.wait()
    for part, copy in enumerate(copies):
        copy.wait()
        result = jnp.dot(rows[...], wbuf[part], preferred_element_type=jnp.float32)
        qkv[:, part * cols : (part + 1) * cols] = result.astype(jnp.bfloat16)
    high_digit = jnp.broadcast_to(pos_ref[...] // BASE, (META, tok))
    low_digit = jnp.broadcast_to(pos_ref[...] % BASE, (META, tok))
    first = lax.broadcasted_iota(jnp.int32, (META, tok), 0) == 0
    chip = lax.axis_index("seq") // PLANE
    for step, refs in enumerate(((kv0_ref, q0_ref), (m1_ref,), (m2_ref,), (m3_ref,))):
        who = jnp.bitwise_xor(chip, step)
        kv_ref = refs[0]
        lo = pl.multiple_of(who * pair, pair)
        query = qkv[:, pl.ds(lo, pair)]
        kv_ref[:tok, :pair] = qkv[:, pl.ds(pl.multiple_of(cols + lo, pair), pair)]
        kv_ref[:tok, pair:] = qkv[:, pl.ds(pl.multiple_of(2 * cols + lo, pair), pair)]
        ids = jnp.where(who >= SPLIT // 2, cid_ref[1:2, :], cid_ref[0:1, :])
        left = jnp.where(first, jnp.broadcast_to(ids, (META, tok)), low_digit)
        kv_ref[tok : tok + META, :pair] = left.astype(jnp.float32).astype(jnp.bfloat16)
        kv_ref[tok : tok + META, pair:] = high_digit.astype(jnp.float32).astype(jnp.bfloat16)
        q_ref, base = (refs[1], 0) if step == 0 else (kv_ref, tok + META)
        q_ref[base : base + tok // 2, :pair] = query[: tok // 2]
        q_ref[base : base + tok // 2, pair:] = query[tok // 2 :]


def project(tokens, positions, cluster_ids, w_query, w_key, w_value):
    tok, depth = tokens.shape
    cols = w_query.shape[1]
    wide = 2 * cols // SPLIT
    vmem = pl.BlockSpec(memory_space=pltpu.VMEM)
    hbm = pl.BlockSpec(memory_space=pltpu.HBM)
    full = tok + META + tok // 2

    def shape(rows):
        return jax.ShapeDtypeStruct((rows, wide), jnp.bfloat16)

    return pl.pallas_call(
        project_kernel,
        out_shape=(shape(tok + META), shape(tok // 2), shape(full), shape(full), shape(full)),
        in_specs=[hbm, vmem, vmem, hbm, hbm, hbm],
        out_specs=(vmem,) * 5,
        scratch_shapes=[
            pltpu.VMEM((tok, depth), jnp.bfloat16),
            pltpu.VMEM((3, depth, cols), jnp.bfloat16),
            pltpu.VMEM((tok, 3 * cols), jnp.bfloat16),
            pltpu.SemaphoreType.DMA((3,)),
            pltpu.SemaphoreType.DMA(()),
        ],
        cost_estimate=pl.CostEstimate(
            flops=6 * tok * depth * cols, bytes_accessed=6 * depth * cols, transcendentals=0
        ),
        name="project",
    )(tokens, positions.reshape(1, tok), cluster_ids, w_query, w_key, w_value)


def pack_kernel(first_ref, second_ref, out_ref):
    half = out_ref.shape[0] // 2
    out_ref[:half, :] = first_ref[:half, :]
    out_ref[half:, :] = second_ref[:half, :]


def pack(first, second, block, flops):
    vmem = pl.BlockSpec(memory_space=pltpu.VMEM)
    wide = first.shape[1]
    return pl.pallas_call(
        pack_kernel,
        out_shape=jax.ShapeDtypeStruct((2 * block, wide), jnp.bfloat16),
        in_specs=[vmem, vmem],
        out_specs=vmem,
        compiler_params=pltpu.CompilerParams(vmem_limit_bytes=PACK_LIMIT),
        cost_estimate=pl.CostEstimate(
            flops=flops, bytes_accessed=8 * block * wide, transcendentals=0
        ),
        name="pack",
    )(first, second)


def ids_of(ref, base, tok, total):
    pair = ref.shape[1] // 2
    cid = ref[base + tok : base + tok + 1, :pair].astype(jnp.float32)
    low = ref[base + tok + 1 : base + tok + 2, :pair].astype(jnp.float32)
    high = ref[base + tok : base + tok + 1, pair:].astype(jnp.float32)
    pos = high * float(BASE) + low
    return cid * float(2 * total) + pos, pos


def unpack(refs, tok, total, keys, values, codes):
    pair = keys.shape[1]
    block = tok + META
    at = 0
    for ref in refs:
        for base in range(0, ref.shape[0], block):
            keys[at : at + tok, :] = ref[base : base + tok, :pair]
            values[at : at + tok, :] = ref[base : base + tok, pair:]
            codes[0:1, at : at + tok] = ids_of(ref, base, tok, total)[0]
            at += tok


def scores_of(q_ref, ids_ref, base, tok, total, keys, codes, column):
    pair = keys.shape[1]
    code, pos = ids_of(ids_ref, base, tok, total)
    column[0:1, :] = code
    column[1:2, :] = pos
    turned = jnp.transpose(column[...])
    gap = turned[:, 0:1] - codes[0:1, :]
    allowed = (gap >= 0.0) & (gap <= turned[:, 1:2])
    bias = jnp.where(allowed, 0.0, -1e30)
    start = q_ref.shape[0] - tok // 2
    query = jnp.concatenate([q_ref[start:, :pair], q_ref[start:, pair:]], axis=0)
    lane = lax.broadcasted_iota(jnp.int32, (tok, pair), 1) < HD
    none = jnp.zeros_like(query)
    both = jnp.concatenate([jnp.where(lane, query, none), jnp.where(lane, none, query)], axis=0)
    scores = lax.dot_general(
        both, keys[...], (((1,), (1,)), ((), ())), preferred_element_type=jnp.float32
    )
    return scores * (HD**-0.5 * LOG2E) + jnp.concatenate([bias, bias], axis=0)


def early_kernel(total, tok, count, *refs):
    q_refs = refs[:SPLIT]
    kv_refs = refs[SPLIT : SPLIT + count]
    expo_ref, stats_ref, values, keys, codes, column = refs[SPLIT + count :]
    unpack(kv_refs, tok, total, keys, values, codes)
    block = tok + META
    for item in range(SPLIT):
        scores = scores_of(
            q_refs[item], kv_refs[item // 2], (item % 2) * block, tok, total, keys, codes, column
        )
        top = jnp.max(scores, axis=1, keepdims=True)
        expo = jnp.exp2(scores - top)
        rows = slice(item * 2 * tok, (item + 1) * 2 * tok)
        expo_ref[rows, :] = expo
        stats_ref[rows, 0:1] = top
        stats_ref[rows, 1:2] = jnp.sum(expo, axis=1, keepdims=True)


def early(total, tok, queries, sources):
    wide = sources[0].shape[1]
    pair = wide // 2
    vmem = pl.BlockSpec(memory_space=pltpu.VMEM)
    count = sum(item.shape[0] for item in sources) // (tok + META) * tok
    rows = 2 * SPLIT * tok
    return pl.pallas_call(
        functools.partial(early_kernel, total, tok, len(sources)),
        out_shape=(
            jax.ShapeDtypeStruct((rows, count), jnp.float32),
            jax.ShapeDtypeStruct((rows, pair), jnp.float32),
            jax.ShapeDtypeStruct((count, pair), jnp.bfloat16),
        ),
        in_specs=[vmem] * (len(queries) + len(sources)),
        out_specs=(vmem,) * 3,
        scratch_shapes=[
            pltpu.VMEM((count, pair), jnp.bfloat16),
            pltpu.VMEM((8, count), jnp.float32),
            pltpu.VMEM((8, tok), jnp.float32),
        ],
        compiler_params=pltpu.CompilerParams(vmem_limit_bytes=ATTEND_LIMIT),
        cost_estimate=pl.CostEstimate(
            flops=EARLY_FLOPS, bytes_accessed=8 * count * pair, transcendentals=rows * count
        ),
        name="early",
    )(*queries, *sources)


def late_kernel(total, tok, item, count, *refs):
    q_ref, ids_ref, expo_ref, stats_ref, old_values = refs[:5]
    kv_refs = refs[5 : 5 + count]
    out_ref, keys, values, codes, column = refs[5 + count :]
    unpack(kv_refs, tok, total, keys, values, codes)
    pair = keys.shape[1]
    scores = scores_of(q_ref, ids_ref, (item % 2) * (tok + META), tok, total, keys, codes, column)
    rows = slice(item * 2 * tok, (item + 1) * 2 * tok)
    old_top = stats_ref[rows, 0:1]
    top = jnp.maximum(jnp.max(scores, axis=1, keepdims=True), old_top)
    expo = jnp.exp2(scores - top)
    factor = jnp.exp2(old_top - top)
    inverse = 1.0 / (jnp.sum(expo, axis=1, keepdims=True) + stats_ref[rows, 1:2] * factor)
    result = jnp.dot(
        (expo_ref[rows, :] * (factor * inverse)).astype(jnp.bfloat16),
        old_values[...],
        preferred_element_type=jnp.float32,
    )
    result += jnp.dot(
        (expo * inverse).astype(jnp.bfloat16), values[...], preferred_element_type=jnp.float32
    )
    lane = lax.broadcasted_iota(jnp.int32, (tok, pair), 1) < HD
    out_ref[...] = jnp.where(lane, result[:tok], result[tok:]).astype(jnp.bfloat16)


def late(total, tok, item, query, ids, expo, stats, old_values, sources):
    pair = old_values.shape[1]
    vmem = pl.BlockSpec(memory_space=pltpu.VMEM)
    count = sum(part.shape[0] for part in sources) // (tok + META) * tok
    return pl.pallas_call(
        functools.partial(late_kernel, total, tok, item, len(sources)),
        out_shape=jax.ShapeDtypeStruct((tok, pair), jnp.bfloat16),
        in_specs=[vmem] * (5 + len(sources)),
        out_specs=vmem,
        scratch_shapes=[
            pltpu.VMEM((count, pair), jnp.bfloat16),
            pltpu.VMEM((count, pair), jnp.bfloat16),
            pltpu.VMEM((8, count), jnp.float32),
            pltpu.VMEM((8, tok), jnp.float32),
        ],
        compiler_params=pltpu.CompilerParams(vmem_limit_bytes=ATTEND_LIMIT),
        cost_estimate=pl.CostEstimate(
            flops=LATE_FLOPS[item], bytes_accessed=4 * count * pair, transcendentals=2 * tok * count
        ),
        name="late",
    )(query, ids, expo, stats, old_values, *sources)


def mix_kernel(*refs):
    own_refs, other_refs = refs[:SPLIT], refs[SPLIT : 2 * SPLIT]
    w_own, w_other, out_ref, left, right = refs[2 * SPLIT :]
    rows, pair = out_ref.shape[0], own_refs[0].shape[1]
    chip = lax.axis_index("seq") // PLANE
    mine = pl.ds(pl.multiple_of(lax.axis_index("head") * rows, rows), rows)
    for step in range(SPLIT):
        lanes = pl.ds(pl.multiple_of(jnp.bitwise_xor(chip, step) * pair, pair), pair)
        left[:, lanes] = own_refs[step][mine, :]
        right[:, lanes] = other_refs[step][mine, :]
    total = jnp.dot(left[...], w_own[...], preferred_element_type=jnp.float32)
    total += jnp.dot(right[...], w_other[...], preferred_element_type=jnp.float32)
    out_ref[...] = total.astype(jnp.bfloat16)


def mix(own, other, w_own, w_other):
    rows = own[0].shape[0] // 2
    deep, width = w_own.shape
    vmem = pl.BlockSpec(memory_space=pltpu.VMEM)
    return pl.pallas_call(
        mix_kernel,
        out_shape=jax.ShapeDtypeStruct((rows, width), jnp.bfloat16),
        in_specs=[vmem] * (2 * SPLIT + 2),
        out_specs=vmem,
        scratch_shapes=[pltpu.VMEM((rows, deep), jnp.bfloat16)] * 2,
        compiler_params=pltpu.CompilerParams(vmem_limit_bytes=PACK_LIMIT),
        cost_estimate=pl.CostEstimate(
            flops=4 * rows * deep * width, bytes_accessed=4 * deep * width, transcendentals=0
        ),
        name="mix",
    )(*own, *other, w_own, w_other)


def per_device_split(tokens, w_query, w_key, w_value, w_out, cluster_ids, positions):
    tok = tokens.shape[0]
    owners = lax.axis_size("seq")
    block = tok + META

    def send(array, bits):
        return lax.ppermute(array, "seq", [(i, i ^ bits) for i in range(owners)])

    def swap(array):
        return lax.ppermute(array, "head", [(0, 1), (1, 0)])

    w_other = swap(w_out)
    kv0, q0, m1, m2, m3 = project(tokens, positions, cluster_ids, w_query, w_key, w_value)
    r1 = send(m1, PLANE)
    r2 = send(m2, 2 * PLANE)
    r3 = send(m3, 3 * PLANE)
    kv0, w_other = lax.optimization_barrier((kv0, w_other))
    near = pack(kv0, r1, block, 0)
    nears = [send(near, bits) for bits in (1, 2, 3)]
    far = pack(r2, r3, block, 10**10)
    far, nears[2] = lax.optimization_barrier((far, nears[2]))
    fars = [send(far, bits) for bits in (1, 2, 3)]
    total = owners * tok
    queries = (q0, r1, r2, r3)
    expo, stats, values = early(total, tok, queries, [near, far, *nears])
    own = [None] * SPLIT
    for item in (3, 2, 1, 0):
        ids = near if item < 2 else far
        part = late(total, tok, item, queries[item], ids, expo, stats, values, fars)
        part, stats = lax.optimization_barrier((part, stats))
        own[item] = send(part, item * PLANE) if item else part
        if item == 1:
            own[3], stats = lax.optimization_barrier((own[3], stats))
    return mix(own, [swap(item) for item in own], w_out, w_other)


def attend_rows(query, keys, values, query_pos, key_pos):
    scores = jnp.einsum("qhd,khd->hqk", query, keys, preferred_element_type=jnp.float32) * HD ** (
        -0.5
    )
    allowed = (key_pos[None, None, :] >= 0) & (key_pos[None, None, :] <= query_pos[None, :, None])
    masked = jnp.where(allowed, scores, jnp.float32(-1e30))
    top = jnp.max(masked, axis=-1, keepdims=True)
    expo = jnp.exp(masked - top)
    weights = (expo / jnp.sum(expo, axis=-1, keepdims=True)).astype(jnp.bfloat16)
    return jnp.einsum("hqk,khd->qhd", weights, values, preferred_element_type=jnp.float32).astype(
        jnp.bfloat16
    )


def attend_group(data, pos):
    rows = data.shape[0]
    width = data.shape[1] // 3
    query = data[:, :width].reshape(rows, GROUP_HEADS, HD)
    keys = data[:, width : 2 * width].reshape(rows, GROUP_HEADS, HD)
    values = data[:, 2 * width :].reshape(rows, GROUP_HEADS, HD)
    half = rows // 2
    first = attend_rows(query[:half], keys, values, pos[:half], pos)
    second = attend_rows(query[half:], keys, values, pos[half:], pos)
    result = jnp.concatenate([first, second], axis=0)
    return result.reshape(rows, width)


def owner_side(pieces):
    data, pos = pieces
    outputs = [attend_group(data[:, item], pos[:, item]) for item in range(data.shape[1])]
    result = jnp.stack(outputs, axis=1)
    return lax.all_to_all(result, "seq", split_axis=0, concat_axis=0, tiled=True)


def per_device_owner(tokens, w_query, w_key, w_value, w_out, cluster_ids, positions):
    tok = tokens.shape[0]
    groups_here = cluster_ids.shape[0]
    owners = lax.axis_size("seq")
    half = tok // 2
    fewer = owners // 4
    capacity = (half + owners - 1) // owners + (half + fewer - 1) // fewer
    slots = owners * capacity
    width = w_query.shape[1] // groups_here
    tok_ids = jnp.arange(tok, dtype=jnp.int32)
    earlier = tok_ids[None, :] < tok_ids[:, None]
    same = cluster_ids[:, :, None] == cluster_ids[:, None, :]
    rank = jnp.sum((same & earlier[None]).astype(jnp.int32), axis=2)
    dest = cluster_ids * capacity + rank
    slot_ids = jnp.arange(slots, dtype=jnp.int32)
    matches = slot_ids[None, :, None] == dest[:, None, :]
    onehot = matches.astype(jnp.bfloat16)
    filled = jnp.any(matches, axis=2)
    pos_sum = jnp.sum(jnp.where(matches, positions[None, None, :], 0), axis=2)
    pos_slots = jnp.where(filled, pos_sum, -1).T

    def project_group(index):
        lo = index * width
        parts = [
            jnp.dot(tokens, weight[:, lo : lo + width], preferred_element_type=jnp.float32).astype(
                jnp.bfloat16
            )
            for weight in (w_query, w_key, w_value)
        ]
        return jnp.concatenate(parts, axis=1)

    data = jnp.stack([project_group(index) for index in range(groups_here)], axis=1)
    send = jnp.einsum("gst,tgc->sgc", onehot, data, preferred_element_type=jnp.float32).astype(
        jnp.bfloat16
    )
    back = owner_side(
        (
            lax.all_to_all(send, "seq", split_axis=0, concat_axis=0, tiled=True),
            lax.all_to_all(pos_slots, "seq", split_axis=0, concat_axis=0, tiled=True),
        )
    )
    attended = jnp.einsum("gst,sgc->tgc", onehot, back, preferred_element_type=jnp.float32).astype(
        jnp.bfloat16
    )
    attended = attended.reshape(tok, groups_here * width)
    mixed = lax.psum_scatter(
        jnp.dot(attended, w_out, preferred_element_type=jnp.float32),
        "head",
        scatter_dimension=0,
        tiled=True,
    )
    return mixed.astype(jnp.bfloat16)


def solution(mesh):
    in_specs = (
        P("seq", None),
        P(None, "head"),
        P(None, "head"),
        P(None, "head"),
        P("head", None),
        P("head", "seq"),
        P("seq"),
    )
    out_specs = P(("seq", "head"), None)
    plan = per_device_split if mesh.shape["seq"] == SPLIT * PLANE else per_device_owner
    return jax.shard_map(
        plan, mesh=mesh, in_specs=in_specs, out_specs=out_specs, check_vma=False
    )
```

```python
import functools

import jax
import jax.numpy as jnp
from jax import lax
from jax.experimental import pallas as pl
from jax.experimental.pallas import tpu as pltpu
from jax.sharding import PartitionSpec as P

HD = 64
GROUP_HEADS = 4

SPLIT = 4
PLANE = 4
META = 8
BASE = 128
PROJECT_LIMIT = (53 << 20) + (512 << 10)
PACK_LIMIT = 4 << 20
ATTEND_LIMIT = 16 << 20
FAR_FLOPS = 10**10
EARLY_FLOPS = 8 * 10**9
LATE_FLOPS = 3 * 10**9
LOG2E = 1.4426950408889634


def project_kernel(steps, tok_hbm, pos_hbm, cid_hbm, wq_ref, wk_ref, wv_ref, *rest):
    out_refs = list(rest[:-6])
    rows, pos_ref, cid_ref, wbuf, sems, small_sems = rest[-6:]
    tok, pair = rows.shape[0], wbuf.shape[2] // 3
    chip = lax.axis_index("seq") // PLANE
    small = [
        pltpu.make_async_copy(source, target, small_sems.at[at])
        for at, (source, target) in enumerate(
            ((tok_hbm, rows), (pos_hbm, pos_ref), (cid_hbm, cid_ref))
        )
    ]
    for copy in small:
        copy.start()
    copies = []
    for at, step in enumerate(steps):
        lanes = pl.ds(pl.multiple_of(jnp.bitwise_xor(chip, step) * pair, pair), pair)
        for part, w_ref in enumerate((wq_ref, wk_ref, wv_ref)):
            target = wbuf.at[at, :, pl.ds(part * pair, pair)]
            copy = pltpu.make_async_copy(w_ref.at[:, lanes], target, sems.at[at, part])
            copy.start()
            copies.append(copy)
    for copy in small:
        copy.wait()
    high_digit = jnp.broadcast_to(pos_ref[...] // BASE, (META, tok))
    low_digit = jnp.broadcast_to(pos_ref[...] % BASE, (META, tok))
    first = lax.broadcasted_iota(jnp.int32, (META, tok), 0) == 0
    for at, step in enumerate(steps):
        for part in range(3):
            copies[3 * at + part].wait()
        result = jnp.dot(rows[...], wbuf[at], preferred_element_type=jnp.float32)
        result = result.astype(jnp.bfloat16)
        kv_ref = out_refs.pop(0)
        kv_ref[:tok, :] = result[:, pair:]
        who = jnp.bitwise_xor(chip, step)
        ids = jnp.where(who >= SPLIT // 2, cid_ref[1:2, :], cid_ref[0:1, :])
        left = jnp.where(first, jnp.broadcast_to(ids, (META, tok)), low_digit)
        kv_ref[tok : tok + META, :pair] = left.astype(jnp.float32).astype(jnp.bfloat16)
        kv_ref[tok : tok + META, pair:] = high_digit.astype(jnp.float32).astype(jnp.bfloat16)
        q_ref, base = (kv_ref, tok + META) if step else (out_refs.pop(0), 0)
        q_ref[base : base + tok // 2, :pair] = result[: tok // 2, :pair]
        q_ref[base : base + tok // 2, pair:] = result[tok // 2 :, :pair]


def project(steps, tokens, positions, cluster_ids, weights):
    tok, depth = tokens.shape
    pair = weights[0].shape[1] // SPLIT
    vmem = pl.BlockSpec(memory_space=pltpu.VMEM)
    hbm = pl.BlockSpec(memory_space=pltpu.HBM)
    sizes = []
    for step in steps:
        sizes += [tok + META + tok // 2] if step else [tok + META, tok // 2]
    return pl.pallas_call(
        functools.partial(project_kernel, steps),
        out_shape=tuple(jax.ShapeDtypeStruct((rows, 2 * pair), jnp.bfloat16) for rows in sizes),
        in_specs=[hbm] * 6,
        out_specs=(vmem,) * len(sizes),
        scratch_shapes=[
            pltpu.VMEM((tok, depth), jnp.bfloat16),
            pltpu.VMEM((1, tok), jnp.int32),
            pltpu.VMEM(cluster_ids.shape, jnp.int32),
            pltpu.VMEM((len(steps), depth, 3 * pair), jnp.bfloat16),
            pltpu.SemaphoreType.DMA((len(steps), 3)),
            pltpu.SemaphoreType.DMA((3,)),
        ],
        compiler_params=pltpu.CompilerParams(vmem_limit_bytes=PROJECT_LIMIT),
        cost_estimate=pl.CostEstimate(
            flops=6 * tok * depth * pair * len(steps),
            bytes_accessed=6 * depth * pair * len(steps),
            transcendentals=0,
        ),
        name="project",
    )(tokens, positions.reshape(1, tok), cluster_ids, *weights)


def pack_kernel(first_ref, second_ref, out_ref):
    half = out_ref.shape[0] // 2
    out_ref[:half, :] = first_ref[:half, :]
    out_ref[half:, :] = second_ref[:half, :]


def pack(first, second, block, flops):
    vmem = pl.BlockSpec(memory_space=pltpu.VMEM)
    wide = first.shape[1]
    return pl.pallas_call(
        pack_kernel,
        out_shape=jax.ShapeDtypeStruct((2 * block, wide), jnp.bfloat16),
        in_specs=[vmem, vmem],
        out_specs=vmem,
        compiler_params=pltpu.CompilerParams(vmem_limit_bytes=PACK_LIMIT),
        cost_estimate=pl.CostEstimate(
            flops=flops, bytes_accessed=8 * block * wide, transcendentals=0
        ),
        name="pack",
    )(first, second)


def ids_of(ref, base, tok, total):
    pair = ref.shape[1] // 2
    cid = ref[base + tok : base + tok + 1, :pair].astype(jnp.float32)
    low = ref[base + tok + 1 : base + tok + 2, :pair].astype(jnp.float32)
    high = ref[base + tok : base + tok + 1, pair:].astype(jnp.float32)
    pos = high * float(BASE) + low
    return cid * float(2 * total) + pos, pos


def unpack(refs, tok, total, keys, values, codes):
    pair = keys.shape[1]
    block = tok + META
    at = 0
    for ref in refs:
        for base in range(0, ref.shape[0], block):
            keys[at : at + tok, :] = ref[base : base + tok, :pair]
            values[at : at + tok, :] = ref[base : base + tok, pair:]
            codes[0:1, at : at + tok] = ids_of(ref, base, tok, total)[0]
            at += tok


def scores_of(q_ref, ids_ref, base, tok, total, keys, codes, column):
    pair = keys.shape[1]
    code, pos = ids_of(ids_ref, base, tok, total)
    column[0:1, :] = code
    column[1:2, :] = pos
    turned = jnp.transpose(column[...])
    gap = turned[:, 0:1] - codes[0:1, :]
    allowed = (gap >= 0.0) & (gap <= turned[:, 1:2])
    bias = jnp.where(allowed, 0.0, -1e30)
    start = q_ref.shape[0] - tok // 2
    query = jnp.concatenate([q_ref[start:, :pair], q_ref[start:, pair:]], axis=0)
    lane = lax.broadcasted_iota(jnp.int32, (tok, pair), 1) < HD
    none = jnp.zeros_like(query)
    both = jnp.concatenate([jnp.where(lane, query, none), jnp.where(lane, none, query)], axis=0)
    scores = lax.dot_general(
        both, keys[...], (((1,), (1,)), ((), ())), preferred_element_type=jnp.float32
    )
    return scores * (HD**-0.5 * LOG2E) + jnp.concatenate([bias, bias], axis=0)


def early_kernel(total, tok, count, *refs):
    q_refs = refs[:SPLIT]
    kv_refs = refs[SPLIT : SPLIT + count]
    expo_ref, stats_ref, values, keys, codes, column = refs[SPLIT + count :]
    unpack(kv_refs, tok, total, keys, values, codes)
    block = tok + META
    for item in range(SPLIT):
        scores = scores_of(
            q_refs[item], kv_refs[item // 2], (item % 2) * block, tok, total, keys, codes, column
        )
        top = jnp.max(scores, axis=1, keepdims=True)
        expo = jnp.exp2(scores - top)
        rows = slice(item * 2 * tok, (item + 1) * 2 * tok)
        expo_ref[rows, :] = expo
        stats_ref[rows, 0:1] = top
        stats_ref[rows, 1:2] = jnp.sum(expo, axis=1, keepdims=True)


def early(total, tok, queries, sources):
    wide = sources[0].shape[1]
    pair = wide // 2
    vmem = pl.BlockSpec(memory_space=pltpu.VMEM)
    count = sum(item.shape[0] for item in sources) // (tok + META) * tok
    rows = 2 * SPLIT * tok
    return pl.pallas_call(
        functools.partial(early_kernel, total, tok, len(sources)),
        out_shape=(
            jax.ShapeDtypeStruct((rows, count), jnp.float32),
            jax.ShapeDtypeStruct((rows, pair), jnp.float32),
            jax.ShapeDtypeStruct((count, pair), jnp.bfloat16),
        ),
        in_specs=[vmem] * (len(queries) + len(sources)),
        out_specs=(vmem,) * 3,
        scratch_shapes=[
            pltpu.VMEM((count, pair), jnp.bfloat16),
            pltpu.VMEM((8, count), jnp.float32),
            pltpu.VMEM((8, tok), jnp.float32),
        ],
        compiler_params=pltpu.CompilerParams(vmem_limit_bytes=ATTEND_LIMIT),
        cost_estimate=pl.CostEstimate(
            flops=EARLY_FLOPS, bytes_accessed=8 * count * pair, transcendentals=rows * count
        ),
        name="early",
    )(*queries, *sources)


def late_kernel(total, tok, items, count, *refs):
    many = len(items)
    q_refs, ids_refs = refs[:many], refs[many : 2 * many]
    expo_ref, stats_ref, old_values = refs[2 * many : 2 * many + 3]
    kv_refs = refs[2 * many + 3 : 2 * many + 3 + count]
    out_refs = refs[2 * many + 3 + count : 3 * many + 3 + count]
    keys, values, codes, column = refs[3 * many + 3 + count :]
    unpack(kv_refs, tok, total, keys, values, codes)
    pair = keys.shape[1]
    lane = lax.broadcasted_iota(jnp.int32, (tok, pair), 1) < HD
    for at, item in enumerate(items):
        base = (item % 2) * (tok + META)
        scores = scores_of(q_refs[at], ids_refs[at], base, tok, total, keys, codes, column)
        rows = slice(item * 2 * tok, (item + 1) * 2 * tok)
        old_top = stats_ref[rows, 0:1]
        top = jnp.maximum(jnp.max(scores, axis=1, keepdims=True), old_top)
        expo = jnp.exp2(scores - top)
        factor = jnp.exp2(old_top - top)
        inverse = 1.0 / (jnp.sum(expo, axis=1, keepdims=True) + stats_ref[rows, 1:2] * factor)
        result = jnp.dot(
            (expo_ref[rows, :] * (factor * inverse)).astype(jnp.bfloat16),
            old_values[...],
            preferred_element_type=jnp.float32,
        )
        result += jnp.dot(
            (expo * inverse).astype(jnp.bfloat16), values[...], preferred_element_type=jnp.float32
        )
        out_refs[at][...] = jnp.where(lane, result[:tok], result[tok:]).astype(jnp.bfloat16)


def late(total, tok, items, queries, ids, expo, stats, old_values, sources):
    pair = old_values.shape[1]
    vmem = pl.BlockSpec(memory_space=pltpu.VMEM)
    count = sum(part.shape[0] for part in sources) // (tok + META) * tok
    return pl.pallas_call(
        functools.partial(late_kernel, total, tok, items, len(sources)),
        out_shape=(jax.ShapeDtypeStruct((tok, pair), jnp.bfloat16),) * len(items),
        in_specs=[vmem] * (2 * len(items) + 3 + len(sources)),
        out_specs=(vmem,) * len(items),
        scratch_shapes=[
            pltpu.VMEM((count, pair), jnp.bfloat16),
            pltpu.VMEM((count, pair), jnp.bfloat16),
            pltpu.VMEM((8, count), jnp.float32),
            pltpu.VMEM((8, tok), jnp.float32),
        ],
        compiler_params=pltpu.CompilerParams(vmem_limit_bytes=ATTEND_LIMIT),
        cost_estimate=pl.CostEstimate(
            flops=LATE_FLOPS,
            bytes_accessed=4 * count * pair,
            transcendentals=2 * len(items) * tok * count,
        ),
        name="late",
    )(*queries, *ids, expo, stats, old_values, *sources)


def mix_kernel(*refs):
    own_refs, other_refs = refs[:SPLIT], refs[SPLIT : 2 * SPLIT]
    w_own, w_other, out_ref, left, right = refs[2 * SPLIT :]
    rows, pair = out_ref.shape[0], own_refs[0].shape[1]
    chip = lax.axis_index("seq") // PLANE
    mine = pl.ds(pl.multiple_of(lax.axis_index("head") * rows, rows), rows)
    for step in range(SPLIT):
        lanes = pl.ds(pl.multiple_of(jnp.bitwise_xor(chip, step) * pair, pair), pair)
        left[:, lanes] = own_refs[step][mine, :]
        right[:, lanes] = other_refs[step][mine, :]
    total = jnp.dot(left[...], w_own[...], preferred_element_type=jnp.float32)
    total += jnp.dot(right[...], w_other[...], preferred_element_type=jnp.float32)
    out_ref[...] = total.astype(jnp.bfloat16)


def mix(own, other, w_own, w_other):
    rows = own[0].shape[0] // 2
    deep, width = w_own.shape
    vmem = pl.BlockSpec(memory_space=pltpu.VMEM)
    return pl.pallas_call(
        mix_kernel,
        out_shape=jax.ShapeDtypeStruct((rows, width), jnp.bfloat16),
        in_specs=[vmem] * (2 * SPLIT + 2),
        out_specs=vmem,
        scratch_shapes=[pltpu.VMEM((rows, deep), jnp.bfloat16)] * 2,
        compiler_params=pltpu.CompilerParams(vmem_limit_bytes=PACK_LIMIT),
        cost_estimate=pl.CostEstimate(
            flops=4 * rows * deep * width, bytes_accessed=4 * deep * width, transcendentals=0
        ),
        name="mix",
    )(*own, *other, w_own, w_other)


def per_device_split(tokens, w_query, w_key, w_value, w_out, cluster_ids, positions):
    tok = tokens.shape[0]
    owners = lax.axis_size("seq")
    block = tok + META

    def send(array, bits):
        return lax.ppermute(array, "seq", [(i, i ^ bits) for i in range(owners)])

    def swap(array):
        return lax.ppermute(array, "head", [(0, 1), (1, 0)])

    w_other = swap(w_out)
    weights = (w_query, w_key, w_value)
    m1, kv0, q0, m3, m2 = project((1, 0, 3, 2), tokens, positions, cluster_ids, weights)
    r1, r3, r2 = send(m1, PLANE), send(m3, 3 * PLANE), send(m2, 2 * PLANE)
    kv0, w_other = lax.optimization_barrier((kv0, w_other))
    near = pack(kv0, r1, block, 0)
    nears = [send(near, bits) for bits in (1, 2, 3)]
    far = pack(r2, r3, block, FAR_FLOPS)
    far, nears[2] = lax.optimization_barrier((far, nears[2]))
    fars = [send(far, bits) for bits in (1, 2, 3)]
    total = owners * tok
    expo, stats, values = early(total, tok, (q0, r1, r2, r3), [near, far, *nears])
    a3, a2 = late(total, tok, (3, 2), (r3, r2), (far, far), expo, stats, values, fars)
    a3, a2, stats = lax.optimization_barrier((a3, a2, stats))
    b3, b2 = send(a3, 3 * PLANE), send(a2, 2 * PLANE)
    a1, a0 = late(total, tok, (1, 0), (r1, q0), (near, near), expo, stats, values, fars)
    a1, b2, b3 = lax.optimization_barrier((a1, b2, b3))
    own = (a0, send(a1, PLANE), b2, b3)
    return mix(own, [swap(item) for item in own], w_out, w_other)


def attend_rows(query, keys, values, query_pos, key_pos):
    scores = jnp.einsum("qhd,khd->hqk", query, keys, preferred_element_type=jnp.float32) * HD ** (
        -0.5
    )
    allowed = (key_pos[None, None, :] >= 0) & (key_pos[None, None, :] <= query_pos[None, :, None])
    masked = jnp.where(allowed, scores, jnp.float32(-1e30))
    top = jnp.max(masked, axis=-1, keepdims=True)
    expo = jnp.exp(masked - top)
    weights = (expo / jnp.sum(expo, axis=-1, keepdims=True)).astype(jnp.bfloat16)
    return jnp.einsum("hqk,khd->qhd", weights, values, preferred_element_type=jnp.float32).astype(
        jnp.bfloat16
    )


def attend_group(data, pos):
    rows = data.shape[0]
    width = data.shape[1] // 3
    query = data[:, :width].reshape(rows, GROUP_HEADS, HD)
    keys = data[:, width : 2 * width].reshape(rows, GROUP_HEADS, HD)
    values = data[:, 2 * width :].reshape(rows, GROUP_HEADS, HD)
    half = rows // 2
    first = attend_rows(query[:half], keys, values, pos[:half], pos)
    second = attend_rows(query[half:], keys, values, pos[half:], pos)
    result = jnp.concatenate([first, second], axis=0)
    return result.reshape(rows, width)


def owner_side(pieces):
    data, pos = pieces
    outputs = [attend_group(data[:, item], pos[:, item]) for item in range(data.shape[1])]
    result = jnp.stack(outputs, axis=1)
    return lax.all_to_all(result, "seq", split_axis=0, concat_axis=0, tiled=True)


def per_device_owner(tokens, w_query, w_key, w_value, w_out, cluster_ids, positions):
    tok = tokens.shape[0]
    groups_here = cluster_ids.shape[0]
    owners = lax.axis_size("seq")
    half = tok // 2
    fewer = owners // 4
    capacity = (half + owners - 1) // owners + (half + fewer - 1) // fewer
    slots = owners * capacity
    width = w_query.shape[1] // groups_here
    tok_ids = jnp.arange(tok, dtype=jnp.int32)
    earlier = tok_ids[None, :] < tok_ids[:, None]
    same = cluster_ids[:, :, None] == cluster_ids[:, None, :]
    rank = jnp.sum((same & earlier[None]).astype(jnp.int32), axis=2)
    dest = cluster_ids * capacity + rank
    slot_ids = jnp.arange(slots, dtype=jnp.int32)
    matches = slot_ids[None, :, None] == dest[:, None, :]
    onehot = matches.astype(jnp.bfloat16)
    filled = jnp.any(matches, axis=2)
    pos_sum = jnp.sum(jnp.where(matches, positions[None, None, :], 0), axis=2)
    pos_slots = jnp.where(filled, pos_sum, -1).T

    def project_group(index):
        lo = index * width
        parts = [
            jnp.dot(tokens, weight[:, lo : lo + width], preferred_element_type=jnp.float32).astype(
                jnp.bfloat16
            )
            for weight in (w_query, w_key, w_value)
        ]
        return jnp.concatenate(parts, axis=1)

    data = jnp.stack([project_group(index) for index in range(groups_here)], axis=1)
    send = jnp.einsum("gst,tgc->sgc", onehot, data, preferred_element_type=jnp.float32).astype(
        jnp.bfloat16
    )
    back = owner_side(
        (
            lax.all_to_all(send, "seq", split_axis=0, concat_axis=0, tiled=True),
            lax.all_to_all(pos_slots, "seq", split_axis=0, concat_axis=0, tiled=True),
        )
    )
    attended = jnp.einsum("gst,sgc->tgc", onehot, back, preferred_element_type=jnp.float32).astype(
        jnp.bfloat16
    )
    attended = attended.reshape(tok, groups_here * width)
    mixed = lax.psum_scatter(
        jnp.dot(attended, w_out, preferred_element_type=jnp.float32),
        "head",
        scatter_dimension=0,
        tiled=True,
    )
    return mixed.astype(jnp.bfloat16)


def solution(mesh):
    in_specs = (
        P("seq", None),
        P(None, "head"),
        P(None, "head"),
        P(None, "head"),
        P("head", None),
        P("head", "seq"),
        P("seq"),
    )
    out_specs = P(("seq", "head"), None)
    plan = per_device_split if mesh.shape["seq"] == SPLIT * PLANE else per_device_owner
    return jax.shard_map(
        plan, mesh=mesh, in_specs=in_specs, out_specs=out_specs, check_vma=False
    )
```

```python
import functools

import jax
import jax.numpy as jnp
from jax import lax
from jax.experimental import pallas as pl
from jax.experimental.pallas import tpu as pltpu
from jax.sharding import PartitionSpec as P

HD = 64
GROUP_HEADS = 4

SPLIT = 4
PLANE = 4
META = 8
BASE = 128
PROJECT_LIMIT = (53 << 20) + (512 << 10)
PACK_LIMIT = 4 << 20
ATTEND_LIMIT = 16 << 20
FAR_FLOPS = 10**10
EARLY_FLOPS = 8 * 10**9
LATE_FLOPS = 3 * 10**9
LOG2E = 1.4426950408889634


def project_kernel(steps, tok_hbm, pos_hbm, cid_hbm, wq_ref, wk_ref, wv_ref, *rest):
    out_refs = list(rest[:-6])
    rows, pos_ref, cid_ref, wbuf, sems, small_sems = rest[-6:]
    tok, pair = rows.shape[0], wbuf.shape[2] // 3
    chip = lax.axis_index("seq") // PLANE
    small = [
        pltpu.make_async_copy(source, target, small_sems.at[at])
        for at, (source, target) in enumerate(
            ((tok_hbm, rows), (pos_hbm, pos_ref), (cid_hbm, cid_ref))
        )
    ]
    for copy in small:
        copy.start()
    copies = []
    for at, step in enumerate(steps):
        lanes = pl.ds(pl.multiple_of(jnp.bitwise_xor(chip, step) * pair, pair), pair)
        for part, w_ref in enumerate((wq_ref, wk_ref, wv_ref)):
            target = wbuf.at[at, :, pl.ds(part * pair, pair)]
            copy = pltpu.make_async_copy(w_ref.at[:, lanes], target, sems.at[at, part])
            copy.start()
            copies.append(copy)
    for copy in small:
        copy.wait()
    high_digit = jnp.broadcast_to(pos_ref[...] // BASE, (META, tok))
    low_digit = jnp.broadcast_to(pos_ref[...] % BASE, (META, tok))
    first = lax.broadcasted_iota(jnp.int32, (META, tok), 0) == 0
    for at, step in enumerate(steps):
        for part in range(3):
            copies[3 * at + part].wait()
        result = jnp.dot(rows[...], wbuf[at], preferred_element_type=jnp.float32)
        result = result.astype(jnp.bfloat16)
        kv_ref = out_refs.pop(0)
        kv_ref[:tok, :] = result[:, pair:]
        who = jnp.bitwise_xor(chip, step)
        ids = jnp.where(who >= SPLIT // 2, cid_ref[1:2, :], cid_ref[0:1, :])
        left = jnp.where(first, jnp.broadcast_to(ids, (META, tok)), low_digit)
        kv_ref[tok : tok + META, :pair] = left.astype(jnp.float32).astype(jnp.bfloat16)
        kv_ref[tok : tok + META, pair:] = high_digit.astype(jnp.float32).astype(jnp.bfloat16)
        q_ref, base = (kv_ref, tok + META) if step else (out_refs.pop(0), 0)
        q_ref[base : base + tok // 2, :pair] = result[: tok // 2, :pair]
        q_ref[base : base + tok // 2, pair:] = result[tok // 2 :, :pair]


def project(steps, tokens, positions, cluster_ids, weights):
    tok, depth = tokens.shape
    pair = weights[0].shape[1] // SPLIT
    vmem = pl.BlockSpec(memory_space=pltpu.VMEM)
    hbm = pl.BlockSpec(memory_space=pltpu.HBM)
    sizes = []
    for step in steps:
        sizes += [tok + META + tok // 2] if step else [tok + META, tok // 2]
    return pl.pallas_call(
        functools.partial(project_kernel, steps),
        out_shape=tuple(jax.ShapeDtypeStruct((rows, 2 * pair), jnp.bfloat16) for rows in sizes),
        in_specs=[hbm] * 6,
        out_specs=(vmem,) * len(sizes),
        scratch_shapes=[
            pltpu.VMEM((tok, depth), jnp.bfloat16),
            pltpu.VMEM((1, tok), jnp.int32),
            pltpu.VMEM(cluster_ids.shape, jnp.int32),
            pltpu.VMEM((len(steps), depth, 3 * pair), jnp.bfloat16),
            pltpu.SemaphoreType.DMA((len(steps), 3)),
            pltpu.SemaphoreType.DMA((3,)),
        ],
        compiler_params=pltpu.CompilerParams(vmem_limit_bytes=PROJECT_LIMIT),
        cost_estimate=pl.CostEstimate(
            flops=6 * tok * depth * pair * len(steps),
            bytes_accessed=6 * depth * pair * len(steps),
            transcendentals=0,
        ),
        name="project",
    )(tokens, *(pltpu.with_memory_space_constraint(x, pltpu.HBM) for x in (positions.reshape(1, tok), cluster_ids)), *weights)


def pack_kernel(first_ref, second_ref, out_ref):
    half = out_ref.shape[0] // 2
    out_ref[:half, :] = first_ref[:half, :]
    out_ref[half:, :] = second_ref[:half, :]


def pack(first, second, block, flops):
    vmem = pl.BlockSpec(memory_space=pltpu.VMEM)
    wide = first.shape[1]
    return pl.pallas_call(
        pack_kernel,
        out_shape=jax.ShapeDtypeStruct((2 * block, wide), jnp.bfloat16),
        in_specs=[vmem, vmem],
        out_specs=vmem,
        compiler_params=pltpu.CompilerParams(vmem_limit_bytes=PACK_LIMIT),
        cost_estimate=pl.CostEstimate(
            flops=flops, bytes_accessed=8 * block * wide, transcendentals=0
        ),
        name="pack",
    )(first, second)


def ids_of(ref, base, tok, total):
    pair = ref.shape[1] // 2
    cid = ref[base + tok : base + tok + 1, :pair].astype(jnp.float32)
    low = ref[base + tok + 1 : base + tok + 2, :pair].astype(jnp.float32)
    high = ref[base + tok : base + tok + 1, pair:].astype(jnp.float32)
    pos = high * float(BASE) + low
    return cid * float(2 * total) + pos, pos


def unpack(refs, tok, total, keys, values, codes):
    pair = keys.shape[1]
    block = tok + META
    at = 0
    for ref in refs:
        for base in range(0, ref.shape[0], block):
            keys[at : at + tok, :] = ref[base : base + tok, :pair]
            values[at : at + tok, :] = ref[base : base + tok, pair:]
            codes[0:1, at : at + tok] = ids_of(ref, base, tok, total)[0]
            at += tok


def scores_of(q_ref, ids_ref, base, tok, total, keys, codes, column):
    pair = keys.shape[1]
    code, pos = ids_of(ids_ref, base, tok, total)
    column[0:1, :] = code
    column[1:2, :] = pos
    turned = jnp.transpose(column[...])
    gap = turned[:, 0:1] - codes[0:1, :]
    allowed = (gap >= 0.0) & (gap <= turned[:, 1:2])
    bias = jnp.where(allowed, 0.0, -1e30)
    start = q_ref.shape[0] - tok // 2
    query = jnp.concatenate([q_ref[start:, :pair], q_ref[start:, pair:]], axis=0)
    lane = lax.broadcasted_iota(jnp.int32, (tok, pair), 1) < HD
    none = jnp.zeros_like(query)
    both = jnp.concatenate([jnp.where(lane, query, none), jnp.where(lane, none, query)], axis=0)
    scores = lax.dot_general(
        both, keys[...], (((1,), (1,)), ((), ())), preferred_element_type=jnp.float32
    )
    return scores * (HD**-0.5 * LOG2E) + jnp.concatenate([bias, bias], axis=0)


def early_kernel(total, tok, count, *refs):
    q_refs = refs[:SPLIT]
    kv_refs = refs[SPLIT : SPLIT + count]
    expo_ref, stats_ref, values, keys, codes, column = refs[SPLIT + count :]
    unpack(kv_refs, tok, total, keys, values, codes)
    block = tok + META
    for item in range(SPLIT):
        scores = scores_of(
            q_refs[item], kv_refs[item // 2], (item % 2) * block, tok, total, keys, codes, column
        )
        top = jnp.max(scores, axis=1, keepdims=True)
        expo = jnp.exp2(scores - top)
        rows = slice(item * 2 * tok, (item + 1) * 2 * tok)
        expo_ref[rows, :] = expo
        stats_ref[rows, 0:1] = top
        stats_ref[rows, 1:2] = jnp.sum(expo, axis=1, keepdims=True)


def early(total, tok, queries, sources):
    wide = sources[0].shape[1]
    pair = wide // 2
    vmem = pl.BlockSpec(memory_space=pltpu.VMEM)
    count = sum(item.shape[0] for item in sources) // (tok + META) * tok
    rows = 2 * SPLIT * tok
    return pl.pallas_call(
        functools.partial(early_kernel, total, tok, len(sources)),
        out_shape=(
            jax.ShapeDtypeStruct((rows, count), jnp.float32),
            jax.ShapeDtypeStruct((rows, pair), jnp.float32),
            jax.ShapeDtypeStruct((count, pair), jnp.bfloat16),
        ),
        in_specs=[vmem] * (len(queries) + len(sources)),
        out_specs=(vmem,) * 3,
        scratch_shapes=[
            pltpu.VMEM((count, pair), jnp.bfloat16),
            pltpu.VMEM((8, count), jnp.float32),
            pltpu.VMEM((8, tok), jnp.float32),
        ],
        compiler_params=pltpu.CompilerParams(vmem_limit_bytes=ATTEND_LIMIT),
        cost_estimate=pl.CostEstimate(
            flops=EARLY_FLOPS, bytes_accessed=8 * count * pair, transcendentals=rows * count
        ),
        name="early",
    )(*queries, *sources)


def late_kernel(total, tok, items, count, *refs):
    many = len(items)
    q_refs, ids_refs = refs[:many], refs[many : 2 * many]
    expo_ref, stats_ref, old_values = refs[2 * many : 2 * many + 3]
    kv_refs = refs[2 * many + 3 : 2 * many + 3 + count]
    out_refs = refs[2 * many + 3 + count : 3 * many + 3 + count]
    keys, values, codes, column = refs[3 * many + 3 + count :]
    unpack(kv_refs, tok, total, keys, values, codes)
    pair = keys.shape[1]
    lane = lax.broadcasted_iota(jnp.int32, (tok, pair), 1) < HD
    for at, item in enumerate(items):
        base = (item % 2) * (tok + META)
        scores = scores_of(q_refs[at], ids_refs[at], base, tok, total, keys, codes, column)
        rows = slice(item * 2 * tok, (item + 1) * 2 * tok)
        old_top = stats_ref[rows, 0:1]
        top = jnp.maximum(jnp.max(scores, axis=1, keepdims=True), old_top)
        expo = jnp.exp2(scores - top)
        factor = jnp.exp2(old_top - top)
        inverse = 1.0 / (jnp.sum(expo, axis=1, keepdims=True) + stats_ref[rows, 1:2] * factor)
        result = jnp.dot(
            (expo_ref[rows, :] * (factor * inverse)).astype(jnp.bfloat16),
            old_values[...],
            preferred_element_type=jnp.float32,
        )
        result += jnp.dot(
            (expo * inverse).astype(jnp.bfloat16), values[...], preferred_element_type=jnp.float32
        )
        out_refs[at][...] = jnp.where(lane, result[:tok], result[tok:]).astype(jnp.bfloat16)


def late(total, tok, items, queries, ids, expo, stats, old_values, sources):
    pair = old_values.shape[1]
    vmem = pl.BlockSpec(memory_space=pltpu.VMEM)
    count = sum(part.shape[0] for part in sources) // (tok + META) * tok
    return pl.pallas_call(
        functools.partial(late_kernel, total, tok, items, len(sources)),
        out_shape=(jax.ShapeDtypeStruct((tok, pair), jnp.bfloat16),) * len(items),
        in_specs=[vmem] * (2 * len(items) + 3 + len(sources)),
        out_specs=(vmem,) * len(items),
        scratch_shapes=[
            pltpu.VMEM((count, pair), jnp.bfloat16),
            pltpu.VMEM((count, pair), jnp.bfloat16),
            pltpu.VMEM((8, count), jnp.float32),
            pltpu.VMEM((8, tok), jnp.float32),
        ],
        compiler_params=pltpu.CompilerParams(vmem_limit_bytes=ATTEND_LIMIT),
        cost_estimate=pl.CostEstimate(
            flops=LATE_FLOPS,
            bytes_accessed=4 * count * pair,
            transcendentals=2 * len(items) * tok * count,
        ),
        name="late",
    )(*queries, *ids, expo, stats, old_values, *sources)


def mix_kernel(*refs):
    own_refs, other_refs = refs[:SPLIT], refs[SPLIT : 2 * SPLIT]
    w_own, w_other, out_ref, left, right = refs[2 * SPLIT :]
    rows, pair = out_ref.shape[0], own_refs[0].shape[1]
    chip = lax.axis_index("seq") // PLANE
    mine = pl.ds(pl.multiple_of(lax.axis_index("head") * rows, rows), rows)
    for step in range(SPLIT):
        lanes = pl.ds(pl.multiple_of(jnp.bitwise_xor(chip, step) * pair, pair), pair)
        left[:, lanes] = own_refs[step][mine, :]
        right[:, lanes] = other_refs[step][mine, :]
    total = jnp.dot(left[...], w_own[...], preferred_element_type=jnp.float32)
    total += jnp.dot(right[...], w_other[...], preferred_element_type=jnp.float32)
    out_ref[...] = total.astype(jnp.bfloat16)


def mix(own, other, w_own, w_other):
    rows = own[0].shape[0] // 2
    deep, width = w_own.shape
    vmem = pl.BlockSpec(memory_space=pltpu.VMEM)
    return pl.pallas_call(
        mix_kernel,
        out_shape=jax.ShapeDtypeStruct((rows, width), jnp.bfloat16),
        in_specs=[vmem] * (2 * SPLIT + 2),
        out_specs=vmem,
        scratch_shapes=[pltpu.VMEM((rows, deep), jnp.bfloat16)] * 2,
        compiler_params=pltpu.CompilerParams(vmem_limit_bytes=PACK_LIMIT),
        cost_estimate=pl.CostEstimate(
            flops=4 * rows * deep * width, bytes_accessed=4 * deep * width, transcendentals=0
        ),
        name="mix",
    )(*own, *other, w_own, w_other)


def per_device_split(tokens, w_query, w_key, w_value, w_out, cluster_ids, positions):
    tok = tokens.shape[0]
    owners = lax.axis_size("seq")
    block = tok + META

    def send(array, bits):
        return lax.ppermute(array, "seq", [(i, i ^ bits) for i in range(owners)])

    def swap(array):
        return lax.ppermute(array, "head", [(0, 1), (1, 0)])

    w_other = swap(w_out)
    weights = (w_query, w_key, w_value)
    m1, kv0, q0, m3, m2 = project((1, 0, 3, 2), tokens, positions, cluster_ids, weights)
    r1, r3, r2 = send(m1, PLANE), send(m3, 3 * PLANE), send(m2, 2 * PLANE)
    kv0, w_other = lax.optimization_barrier((kv0, w_other))
    near = pack(kv0, r1, block, 0)
    nears = [send(near, bits) for bits in (1, 2, 3)]
    far = pack(r2, r3, block, FAR_FLOPS)
    far, nears[2] = lax.optimization_barrier((far, nears[2]))
    fars = [send(far, bits) for bits in (1, 2, 3)]
    total = owners * tok
    expo, stats, values = early(total, tok, (q0, r1, r2, r3), [near, far, *nears])
    queries, own = (q0, r1, r2, r3), [None] * SPLIT
    for item in (3, 2, 1, 0):
        ids = near if item < 2 else far
        (part,) = late(total, tok, (item,), (queries[item],), (ids,), expo, stats, values, fars)
        part, stats = lax.optimization_barrier((part, stats))
        own[item] = part
    own[3], own[2] = lax.optimization_barrier((own[3], own[2]))
    b3 = send(own[3], 3 * PLANE)
    own = (own[0], send(own[1], PLANE), send(own[2], 2 * PLANE), b3)
    return mix(own, [swap(item) for item in own], w_out, w_other)


def attend_rows(query, keys, values, query_pos, key_pos):
    scores = jnp.einsum("qhd,khd->hqk", query, keys, preferred_element_type=jnp.float32) * HD ** (
        -0.5
    )
    allowed = (key_pos[None, None, :] >= 0) & (key_pos[None, None, :] <= query_pos[None, :, None])
    masked = jnp.where(allowed, scores, jnp.float32(-1e30))
    top = jnp.max(masked, axis=-1, keepdims=True)
    expo = jnp.exp(masked - top)
    weights = (expo / jnp.sum(expo, axis=-1, keepdims=True)).astype(jnp.bfloat16)
    return jnp.einsum("hqk,khd->qhd", weights, values, preferred_element_type=jnp.float32).astype(
        jnp.bfloat16
    )


def attend_group(data, pos):
    rows = data.shape[0]
    width = data.shape[1] // 3
    query = data[:, :width].reshape(rows, GROUP_HEADS, HD)
    keys = data[:, width : 2 * width].reshape(rows, GROUP_HEADS, HD)
    values = data[:, 2 * width :].reshape(rows, GROUP_HEADS, HD)
    half = rows // 2
    first = attend_rows(query[:half], keys, values, pos[:half], pos)
    second = attend_rows(query[half:], keys, values, pos[half:], pos)
    result = jnp.concatenate([first, second], axis=0)
    return result.reshape(rows, width)


def owner_side(pieces):
    data, pos = pieces
    outputs = [attend_group(data[:, item], pos[:, item]) for item in range(data.shape[1])]
    result = jnp.stack(outputs, axis=1)
    return lax.all_to_all(result, "seq", split_axis=0, concat_axis=0, tiled=True)


def per_device_owner(tokens, w_query, w_key, w_value, w_out, cluster_ids, positions):
    tok = tokens.shape[0]
    groups_here = cluster_ids.shape[0]
    owners = lax.axis_size("seq")
    half = tok // 2
    fewer = owners // 4
    capacity = (half + owners - 1) // owners + (half + fewer - 1) // fewer
    slots = owners * capacity
    width = w_query.shape[1] // groups_here
    tok_ids = jnp.arange(tok, dtype=jnp.int32)
    earlier = tok_ids[None, :] < tok_ids[:, None]
    same = cluster_ids[:, :, None] == cluster_ids[:, None, :]
    rank = jnp.sum((same & earlier[None]).astype(jnp.int32), axis=2)
    dest = cluster_ids * capacity + rank
    slot_ids = jnp.arange(slots, dtype=jnp.int32)
    matches = slot_ids[None, :, None] == dest[:, None, :]
    onehot = matches.astype(jnp.bfloat16)
    filled = jnp.any(matches, axis=2)
    pos_sum = jnp.sum(jnp.where(matches, positions[None, None, :], 0), axis=2)
    pos_slots = jnp.where(filled, pos_sum, -1).T

    def project_group(index):
        lo = index * width
        parts = [
            jnp.dot(tokens, weight[:, lo : lo + width], preferred_element_type=jnp.float32).astype(
                jnp.bfloat16
            )
            for weight in (w_query, w_key, w_value)
        ]
        return jnp.concatenate(parts, axis=1)

    data = jnp.stack([project_group(index) for index in range(groups_here)], axis=1)
    send = jnp.einsum("gst,tgc->sgc", onehot, data, preferred_element_type=jnp.float32).astype(
        jnp.bfloat16
    )
    back = owner_side(
        (
            lax.all_to_all(send, "seq", split_axis=0, concat_axis=0, tiled=True),
            lax.all_to_all(pos_slots, "seq", split_axis=0, concat_axis=0, tiled=True),
        )
    )
    attended = jnp.einsum("gst,sgc->tgc", onehot, back, preferred_element_type=jnp.float32).astype(
        jnp.bfloat16
    )
    attended = attended.reshape(tok, groups_here * width)
    mixed = lax.psum_scatter(
        jnp.dot(attended, w_out, preferred_element_type=jnp.float32),
        "head",
        scatter_dimension=0,
        tiled=True,
    )
    return mixed.astype(jnp.bfloat16)


def solution(mesh):
    in_specs = (
        P("seq", None),
        P(None, "head"),
        P(None, "head"),
        P(None, "head"),
        P("head", None),
        P("head", "seq"),
        P("seq"),
    )
    out_specs = P(("seq", "head"), None)
    plan = per_device_split if mesh.shape["seq"] == SPLIT * PLANE else per_device_owner
    return jax.shard_map(
        plan, mesh=mesh, in_specs=in_specs, out_specs=out_specs, check_vma=False
    )
```

```python
import functools

import jax
import jax.numpy as jnp
from jax import lax
from jax.experimental import pallas as pl
from jax.experimental.pallas import tpu as pltpu
from jax.sharding import PartitionSpec as P

HD = 64
GROUP_HEADS = 4

SPLIT = 4
PLANE = 4
META = 8
BASE = 128
PROJECT_LIMIT = (53 << 20) + (512 << 10)
PACK_LIMIT = 4 << 20
ATTEND_LIMIT = 16 << 20
FAR_FLOPS = 10**10
EARLY_FLOPS = 8 * 10**9
LATE_FLOPS = 3 * 10**9
LOG2E = 1.4426950408889634


def project_kernel(steps, tok_hbm, pos_hbm, cid_hbm, wq_ref, wk_ref, wv_ref, *rest):
    out_refs = list(rest[:-6])
    rows, pos_ref, cid_ref, wbuf, sems, small_sems = rest[-6:]
    tok, pair = rows.shape[0], wbuf.shape[2] // 3
    chip = lax.axis_index("seq") // PLANE
    small = [
        pltpu.make_async_copy(source, target, small_sems.at[at])
        for at, (source, target) in enumerate(
            ((tok_hbm, rows), (pos_hbm, pos_ref), (cid_hbm, cid_ref))
        )
    ]
    for copy in small:
        copy.start()
    copies = []
    for at, step in enumerate(steps):
        lanes = pl.ds(pl.multiple_of(jnp.bitwise_xor(chip, step) * pair, pair), pair)
        for part, w_ref in enumerate((wq_ref, wk_ref, wv_ref)):
            target = wbuf.at[at, :, pl.ds(part * pair, pair)]
            copy = pltpu.make_async_copy(w_ref.at[:, lanes], target, sems.at[at, part])
            copy.start()
            copies.append(copy)
    for copy in small:
        copy.wait()
    high_digit = jnp.broadcast_to(pos_ref[...] // BASE, (META, tok))
    low_digit = jnp.broadcast_to(pos_ref[...] % BASE, (META, tok))
    first = lax.broadcasted_iota(jnp.int32, (META, tok), 0) == 0
    for at, step in enumerate(steps):
        for part in range(3):
            copies[3 * at + part].wait()
        result = jnp.dot(rows[...], wbuf[at], preferred_element_type=jnp.float32)
        result = result.astype(jnp.bfloat16)
        kv_ref = out_refs.pop(0)
        kv_ref[:tok, :] = result[:, pair:]
        who = jnp.bitwise_xor(chip, step)
        ids = jnp.where(who >= SPLIT // 2, cid_ref[1:2, :], cid_ref[0:1, :])
        left = jnp.where(first, jnp.broadcast_to(ids, (META, tok)), low_digit)
        kv_ref[tok : tok + META, :pair] = left.astype(jnp.float32).astype(jnp.bfloat16)
        kv_ref[tok : tok + META, pair:] = high_digit.astype(jnp.float32).astype(jnp.bfloat16)
        q_ref, base = (kv_ref, tok + META) if step else (out_refs.pop(0), 0)
        q_ref[base : base + tok // 2, :pair] = result[: tok // 2, :pair]
        q_ref[base : base + tok // 2, pair:] = result[tok // 2 :, :pair]


def project(steps, tokens, positions, cluster_ids, weights):
    tok, depth = tokens.shape
    pair = weights[0].shape[1] // SPLIT
    vmem = pl.BlockSpec(memory_space=pltpu.VMEM)
    hbm = pl.BlockSpec(memory_space=pltpu.HBM)
    sizes = []
    for step in steps:
        sizes += [tok + META + tok // 2] if step else [tok + META, tok // 2]
    return pl.pallas_call(
        functools.partial(project_kernel, steps),
        out_shape=tuple(jax.ShapeDtypeStruct((rows, 2 * pair), jnp.bfloat16) for rows in sizes),
        in_specs=[hbm] * 6,
        out_specs=(vmem,) * len(sizes),
        scratch_shapes=[
            pltpu.VMEM((tok, depth), jnp.bfloat16),
            pltpu.VMEM((1, tok), jnp.int32),
            pltpu.VMEM(cluster_ids.shape, jnp.int32),
            pltpu.VMEM((len(steps), depth, 3 * pair), jnp.bfloat16),
            pltpu.SemaphoreType.DMA((len(steps), 3)),
            pltpu.SemaphoreType.DMA((3,)),
        ],
        compiler_params=pltpu.CompilerParams(vmem_limit_bytes=PROJECT_LIMIT),
        cost_estimate=pl.CostEstimate(
            flops=6 * tok * depth * pair * len(steps),
            bytes_accessed=6 * depth * pair * len(steps),
            transcendentals=0,
        ),
        name="project",
    )(tokens, *(pltpu.with_memory_space_constraint(x, pltpu.HBM) for x in (positions.reshape(1, tok), cluster_ids)), *weights)


def pack_kernel(first_ref, second_ref, out_ref):
    tok = (out_ref.shape[0] - META) // 2
    out_ref[:tok, :] = first_ref[:tok, :]
    out_ref[tok : 2 * tok, :] = second_ref[:tok, :]
    first = first_ref[tok : tok + META, :].astype(jnp.float32)
    second = second_ref[tok : tok + META, :].astype(jnp.float32)
    row = lax.broadcasted_iota(jnp.int32, first.shape, 0)
    low = jnp.broadcast_to(second[1:2], first.shape)
    second = jnp.where(row == META // 2, jnp.broadcast_to(second[0:1], first.shape), low)
    out_ref[2 * tok :, :] = jnp.where(row < META // 2, first, second).astype(jnp.bfloat16)


def pack(first, second, tok, flops):
    vmem = pl.BlockSpec(memory_space=pltpu.VMEM)
    wide = first.shape[1]
    return pl.pallas_call(
        pack_kernel,
        out_shape=jax.ShapeDtypeStruct((2 * tok + META, wide), jnp.bfloat16),
        in_specs=[vmem, vmem],
        out_specs=vmem,
        compiler_params=pltpu.CompilerParams(vmem_limit_bytes=PACK_LIMIT),
        cost_estimate=pl.CostEstimate(
            flops=flops, bytes_accessed=8 * tok * wide, transcendentals=0
        ),
        name="pack",
    )(first, second)


def ids_of(ref, item, tok, total):
    pair = ref.shape[1] // 2
    row = 2 * tok + item * (META // 2)
    cid = ref[row : row + 1, :pair].astype(jnp.float32)
    low = ref[row + 1 : row + 2, :pair].astype(jnp.float32)
    high = ref[row : row + 1, pair:].astype(jnp.float32)
    pos = high * float(BASE) + low
    return cid * float(2 * total) + pos, pos


def unpack(refs, tok, total, keys, values, codes):
    pair = keys.shape[1]
    for at, ref in enumerate(refs):
        rows = slice(2 * at * tok, 2 * (at + 1) * tok)
        keys[rows, :] = ref[: 2 * tok, :pair]
        values[rows, :] = ref[: 2 * tok, pair:]
        for item in range(2):
            start = (2 * at + item) * tok
            codes[0:1, start : start + tok] = ids_of(ref, item, tok, total)[0]


def scores_of(q_ref, ids_ref, which, tok, total, keys, codes, column):
    pair = keys.shape[1]
    code, pos = ids_of(ids_ref, which, tok, total)
    column[0:1, :] = code
    column[1:2, :] = pos
    turned = jnp.transpose(column[...])
    gap = turned[:, 0:1] - codes[0:1, :]
    allowed = (gap >= 0.0) & (gap <= turned[:, 1:2])
    bias = jnp.where(allowed, 0.0, -1e30)
    start = q_ref.shape[0] - tok // 2
    query = jnp.concatenate([q_ref[start:, :pair], q_ref[start:, pair:]], axis=0)
    lane = lax.broadcasted_iota(jnp.int32, (tok, pair), 1) < HD
    none = jnp.zeros_like(query)
    both = jnp.concatenate([jnp.where(lane, query, none), jnp.where(lane, none, query)], axis=0)
    scores = lax.dot_general(
        both, keys[...], (((1,), (1,)), ((), ())), preferred_element_type=jnp.float32
    )
    return scores * (HD**-0.5 * LOG2E) + jnp.concatenate([bias, bias], axis=0)


def early_kernel(total, tok, count, *refs):
    q_refs = refs[:SPLIT]
    kv_refs = refs[SPLIT : SPLIT + count]
    expo_ref, stats_ref, values, keys, codes, column = refs[SPLIT + count :]
    unpack(kv_refs, tok, total, keys, values, codes)
    for item in range(SPLIT):
        scores = scores_of(
            q_refs[item], kv_refs[item // 2], item % 2, tok, total, keys, codes, column
        )
        top = jnp.max(scores, axis=1, keepdims=True)
        expo = jnp.exp2(scores - top)
        rows = slice(item * 2 * tok, (item + 1) * 2 * tok)
        expo_ref[rows, :] = expo
        stats_ref[rows, 0:1] = top
        stats_ref[rows, 1:2] = jnp.sum(expo, axis=1, keepdims=True)


def early(total, tok, queries, sources):
    wide = sources[0].shape[1]
    pair = wide // 2
    vmem = pl.BlockSpec(memory_space=pltpu.VMEM)
    count = 2 * tok * len(sources)
    rows = 2 * SPLIT * tok
    return pl.pallas_call(
        functools.partial(early_kernel, total, tok, len(sources)),
        out_shape=(
            jax.ShapeDtypeStruct((rows, count), jnp.float32),
            jax.ShapeDtypeStruct((rows, pair), jnp.float32),
            jax.ShapeDtypeStruct((count, pair), jnp.bfloat16),
        ),
        in_specs=[vmem] * (len(queries) + len(sources)),
        out_specs=(vmem,) * 3,
        scratch_shapes=[
            pltpu.VMEM((count, pair), jnp.bfloat16),
            pltpu.VMEM((8, count), jnp.float32),
            pltpu.VMEM((8, tok), jnp.float32),
        ],
        compiler_params=pltpu.CompilerParams(vmem_limit_bytes=ATTEND_LIMIT),
        cost_estimate=pl.CostEstimate(
            flops=EARLY_FLOPS, bytes_accessed=8 * count * pair, transcendentals=rows * count
        ),
        name="early",
    )(*queries, *sources)


def late_kernel(total, tok, items, count, *refs):
    many = len(items)
    q_refs, ids_refs = refs[:many], refs[many : 2 * many]
    expo_ref, stats_ref, old_values = refs[2 * many : 2 * many + 3]
    kv_refs = refs[2 * many + 3 : 2 * many + 3 + count]
    out_refs = refs[2 * many + 3 + count : 3 * many + 3 + count]
    keys, values, codes, column = refs[3 * many + 3 + count :]
    unpack(kv_refs, tok, total, keys, values, codes)
    pair = keys.shape[1]
    lane = lax.broadcasted_iota(jnp.int32, (tok, pair), 1) < HD
    for at, item in enumerate(items):
        scores = scores_of(q_refs[at], ids_refs[at], item % 2, tok, total, keys, codes, column)
        rows = slice(item * 2 * tok, (item + 1) * 2 * tok)
        old_top = stats_ref[rows, 0:1]
        top = jnp.maximum(jnp.max(scores, axis=1, keepdims=True), old_top)
        expo = jnp.exp2(scores - top)
        factor = jnp.exp2(old_top - top)
        inverse = 1.0 / (jnp.sum(expo, axis=1, keepdims=True) + stats_ref[rows, 1:2] * factor)
        result = jnp.dot(
            (expo_ref[rows, :] * (factor * inverse)).astype(jnp.bfloat16),
            old_values[...],
            preferred_element_type=jnp.float32,
        )
        result += jnp.dot(
            (expo * inverse).astype(jnp.bfloat16), values[...], preferred_element_type=jnp.float32
        )
        out_refs[at][...] = jnp.where(lane, result[:tok], result[tok:]).astype(jnp.bfloat16)


def late(total, tok, items, queries, ids, expo, stats, old_values, sources):
    pair = old_values.shape[1]
    vmem = pl.BlockSpec(memory_space=pltpu.VMEM)
    count = 2 * tok * len(sources)
    return pl.pallas_call(
        functools.partial(late_kernel, total, tok, items, len(sources)),
        out_shape=(jax.ShapeDtypeStruct((tok, pair), jnp.bfloat16),) * len(items),
        in_specs=[vmem] * (2 * len(items) + 3 + len(sources)),
        out_specs=(vmem,) * len(items),
        scratch_shapes=[
            pltpu.VMEM((count, pair), jnp.bfloat16),
            pltpu.VMEM((count, pair), jnp.bfloat16),
            pltpu.VMEM((8, count), jnp.float32),
            pltpu.VMEM((8, tok), jnp.float32),
        ],
        compiler_params=pltpu.CompilerParams(vmem_limit_bytes=ATTEND_LIMIT),
        cost_estimate=pl.CostEstimate(
            flops=LATE_FLOPS,
            bytes_accessed=4 * count * pair,
            transcendentals=2 * len(items) * tok * count,
        ),
        name="late",
    )(*queries, *ids, expo, stats, old_values, *sources)


def mix_kernel(with_sum, *refs):
    piece_refs, (w_ref, *sum_refs, out_ref, rows_buf) = refs[:SPLIT], refs[SPLIT:]
    rows, pair = out_ref.shape[0], piece_refs[0].shape[1]
    chip = lax.axis_index("seq") // PLANE
    mine = pl.ds(pl.multiple_of(lax.axis_index("head") * rows, rows), rows)
    for step in range(SPLIT):
        lanes = pl.ds(pl.multiple_of(jnp.bitwise_xor(chip, step) * pair, pair), pair)
        rows_buf[:, lanes] = piece_refs[step][mine, :]
    total = jnp.dot(rows_buf[...], w_ref[...], preferred_element_type=jnp.float32)
    if with_sum:
        total += sum_refs[0][...]
    out_ref[...] = total.astype(out_ref.dtype)


def mix(pieces, weight, before=None):
    rows = pieces[0].shape[0] // 2
    deep, width = weight.shape
    vmem = pl.BlockSpec(memory_space=pltpu.VMEM)
    sums = [] if before is None else [before]
    dtype = jnp.float32 if before is None else jnp.bfloat16
    return pl.pallas_call(
        functools.partial(mix_kernel, before is not None),
        out_shape=jax.ShapeDtypeStruct((rows, width), dtype),
        in_specs=[vmem] * (SPLIT + 1 + len(sums)),
        out_specs=vmem,
        scratch_shapes=[pltpu.VMEM((rows, deep), jnp.bfloat16)],
        compiler_params=pltpu.CompilerParams(vmem_limit_bytes=PACK_LIMIT),
        cost_estimate=pl.CostEstimate(
            flops=2 * rows * deep * width, bytes_accessed=2 * deep * width, transcendentals=0
        ),
        name="mix",
    )(*pieces, weight, *sums)


def per_device_split(tokens, w_query, w_key, w_value, w_out, cluster_ids, positions):
    tok = tokens.shape[0]
    owners = lax.axis_size("seq")

    def send(array, bits):
        return lax.ppermute(array, "seq", [(i, i ^ bits) for i in range(owners)])

    def swap(array):
        return lax.ppermute(array, "head", [(0, 1), (1, 0)])

    w_other = swap(w_out)
    weights = (w_query, w_key, w_value)
    m1, kv0, q0, m3, m2 = project((1, 0, 3, 2), tokens, positions, cluster_ids, weights)
    r1, r3, r2 = send(m1, PLANE), send(m3, 3 * PLANE), send(m2, 2 * PLANE)
    kv0, w_other = lax.optimization_barrier((kv0, w_other))
    near = pack(kv0, r1, tok, 0)
    nears = [send(near, bits) for bits in (1, 2, 3)]
    far = pack(r2, r3, tok, FAR_FLOPS)
    far, nears[1] = lax.optimization_barrier((far, nears[1]))
    fars = [send(far, bits) for bits in (1, 2, 3)]
    total = owners * tok
    expo, stats, values = early(total, tok, (q0, r1, r2, r3), [near, far, *nears])
    queries, own = (q0, r1, r2, r3), [None] * SPLIT
    for item in (3, 2, 1, 0):
        ids = near if item < 2 else far
        (part,) = late(total, tok, (item,), (queries[item],), (ids,), expo, stats, values, fars)
        part, stats = lax.optimization_barrier((part, stats))
        own[item] = part
    own[3], own[2] = lax.optimization_barrier((own[3], own[2]))
    b3 = send(own[3], 3 * PLANE)
    own = (own[0], send(own[1], PLANE), send(own[2], 2 * PLANE), b3)
    half = mix(own, w_out)
    return mix([swap(item) for item in own], w_other, half)


def attend_rows(query, keys, values, query_pos, key_pos):
    scores = jnp.einsum("qhd,khd->hqk", query, keys, preferred_element_type=jnp.float32) * HD ** (
        -0.5
    )
    allowed = (key_pos[None, None, :] >= 0) & (key_pos[None, None, :] <= query_pos[None, :, None])
    masked = jnp.where(allowed, scores, jnp.float32(-1e30))
    top = jnp.max(masked, axis=-1, keepdims=True)
    expo = jnp.exp(masked - top)
    weights = (expo / jnp.sum(expo, axis=-1, keepdims=True)).astype(jnp.bfloat16)
    return jnp.einsum("hqk,khd->qhd", weights, values, preferred_element_type=jnp.float32).astype(
        jnp.bfloat16
    )


def attend_group(data, pos):
    rows = data.shape[0]
    width = data.shape[1] // 3
    query = data[:, :width].reshape(rows, GROUP_HEADS, HD)
    keys = data[:, width : 2 * width].reshape(rows, GROUP_HEADS, HD)
    values = data[:, 2 * width :].reshape(rows, GROUP_HEADS, HD)
    half = rows // 2
    first = attend_rows(query[:half], keys, values, pos[:half], pos)
    second = attend_rows(query[half:], keys, values, pos[half:], pos)
    result = jnp.concatenate([first, second], axis=0)
    return result.reshape(rows, width)


def owner_side(pieces):
    data, pos = pieces
    outputs = [attend_group(data[:, item], pos[:, item]) for item in range(data.shape[1])]
    result = jnp.stack(outputs, axis=1)
    return lax.all_to_all(result, "seq", split_axis=0, concat_axis=0, tiled=True)


def per_device_owner(tokens, w_query, w_key, w_value, w_out, cluster_ids, positions):
    tok = tokens.shape[0]
    groups_here = cluster_ids.shape[0]
    owners = lax.axis_size("seq")
    half = tok // 2
    fewer = owners // 4
    capacity = (half + owners - 1) // owners + (half + fewer - 1) // fewer
    slots = owners * capacity
    width = w_query.shape[1] // groups_here
    tok_ids = jnp.arange(tok, dtype=jnp.int32)
    earlier = tok_ids[None, :] < tok_ids[:, None]
    same = cluster_ids[:, :, None] == cluster_ids[:, None, :]
    rank = jnp.sum((same & earlier[None]).astype(jnp.int32), axis=2)
    dest = cluster_ids * capacity + rank
    slot_ids = jnp.arange(slots, dtype=jnp.int32)
    matches = slot_ids[None, :, None] == dest[:, None, :]
    onehot = matches.astype(jnp.bfloat16)
    filled = jnp.any(matches, axis=2)
    pos_sum = jnp.sum(jnp.where(matches, positions[None, None, :], 0), axis=2)
    pos_slots = jnp.where(filled, pos_sum, -1).T

    def project_group(index):
        lo = index * width
        parts = [
            jnp.dot(tokens, weight[:, lo : lo + width], preferred_element_type=jnp.float32).astype(
                jnp.bfloat16
            )
            for weight in (w_query, w_key, w_value)
        ]
        return jnp.concatenate(parts, axis=1)

    data = jnp.stack([project_group(index) for index in range(groups_here)], axis=1)
    send = jnp.einsum("gst,tgc->sgc", onehot, data, preferred_element_type=jnp.float32).astype(
        jnp.bfloat16
    )
    back = owner_side(
        (
            lax.all_to_all(send, "seq", split_axis=0, concat_axis=0, tiled=True),
            lax.all_to_all(pos_slots, "seq", split_axis=0, concat_axis=0, tiled=True),
        )
    )
    attended = jnp.einsum("gst,sgc->tgc", onehot, back, preferred_element_type=jnp.float32).astype(
        jnp.bfloat16
    )
    attended = attended.reshape(tok, groups_here * width)
    mixed = lax.psum_scatter(
        jnp.dot(attended, w_out, preferred_element_type=jnp.float32),
        "head",
        scatter_dimension=0,
        tiled=True,
    )
    return mixed.astype(jnp.bfloat16)


def solution(mesh):
    in_specs = (
        P("seq", None),
        P(None, "head"),
        P(None, "head"),
        P(None, "head"),
        P("head", None),
        P("head", "seq"),
        P("seq"),
    )
    out_specs = P(("seq", "head"), None)
    plan = per_device_split if mesh.shape["seq"] == SPLIT * PLANE else per_device_owner
    return jax.shard_map(
        plan, mesh=mesh, in_specs=in_specs, out_specs=out_specs, check_vma=False
    )
```

```python
import functools

import jax
import jax.numpy as jnp
from jax import lax
from jax.experimental import pallas as pl
from jax.experimental.pallas import tpu as pltpu
from jax.sharding import PartitionSpec as P

HD = 64
GROUP_HEADS = 4

SPLIT = 4
PLANE = 4
META = 8
BASE = 128
PROJECT_LIMIT = (53 << 20) + (512 << 10)
PACK_LIMIT = 4 << 20
ATTEND_LIMIT = 16 << 20
FAR_FLOPS = 10**10
EARLY_FLOPS = 8 * 10**9
LATE_FLOPS = 3 * 10**9
LOG2E = 1.4426950408889634


def project_kernel(steps, tok_hbm, pos_hbm, cid_hbm, wq_ref, wk_ref, wv_ref, *rest):
    out_refs = list(rest[:-6])
    rows, pos_ref, cid_ref, wbuf, sems, small_sems = rest[-6:]
    tok, pair = rows.shape[0], wbuf.shape[2] // 3
    chip = lax.axis_index("seq") // PLANE
    small = [
        pltpu.make_async_copy(source, target, small_sems.at[at])
        for at, (source, target) in enumerate(
            ((tok_hbm, rows), (pos_hbm, pos_ref), (cid_hbm, cid_ref))
        )
    ]
    for copy in small:
        copy.start()
    copies = []
    for at, step in enumerate(steps):
        lanes = pl.ds(pl.multiple_of(jnp.bitwise_xor(chip, step) * pair, pair), pair)
        for part, w_ref in enumerate((wq_ref, wk_ref, wv_ref)):
            target = wbuf.at[at, :, pl.ds(part * pair, pair)]
            copy = pltpu.make_async_copy(w_ref.at[:, lanes], target, sems.at[at, part])
            copy.start()
            copies.append(copy)
    for copy in small:
        copy.wait()
    high_digit = jnp.broadcast_to(pos_ref[...] // BASE, (META, tok))
    low_digit = jnp.broadcast_to(pos_ref[...] % BASE, (META, tok))
    first = lax.broadcasted_iota(jnp.int32, (META, tok), 0) == 0
    for at, step in enumerate(steps):
        for part in range(3):
            copies[3 * at + part].wait()
        result = jnp.dot(rows[...], wbuf[at], preferred_element_type=jnp.float32)
        result = result.astype(jnp.bfloat16)
        kv_ref = out_refs.pop(0)
        kv_ref[:tok, :] = result[:, pair:]
        who = jnp.bitwise_xor(chip, step)
        ids = jnp.where(who >= SPLIT // 2, cid_ref[1:2, :], cid_ref[0:1, :])
        left = jnp.where(first, jnp.broadcast_to(ids, (META, tok)), low_digit)
        kv_ref[tok : tok + META, :pair] = left.astype(jnp.float32).astype(jnp.bfloat16)
        kv_ref[tok : tok + META, pair:] = high_digit.astype(jnp.float32).astype(jnp.bfloat16)
        q_ref, base = (kv_ref, tok + META) if step else (out_refs.pop(0), 0)
        q_ref[base : base + tok // 2, :pair] = result[: tok // 2, :pair]
        q_ref[base : base + tok // 2, pair:] = result[tok // 2 :, :pair]


def project(steps, tokens, positions, cluster_ids, weights):
    tok, depth = tokens.shape
    pair = weights[0].shape[1] // SPLIT
    vmem = pl.BlockSpec(memory_space=pltpu.VMEM)
    hbm = pl.BlockSpec(memory_space=pltpu.HBM)
    sizes = []
    for step in steps:
        sizes += [tok + META + tok // 2] if step else [tok + META, tok // 2]
    return pl.pallas_call(
        functools.partial(project_kernel, steps),
        out_shape=tuple(jax.ShapeDtypeStruct((rows, 2 * pair), jnp.bfloat16) for rows in sizes),
        in_specs=[hbm] * 6,
        out_specs=(vmem,) * len(sizes),
        scratch_shapes=[
            pltpu.VMEM((tok, depth), jnp.bfloat16),
            pltpu.VMEM((1, tok), jnp.int32),
            pltpu.VMEM(cluster_ids.shape, jnp.int32),
            pltpu.VMEM((len(steps), depth, 3 * pair), jnp.bfloat16),
            pltpu.SemaphoreType.DMA((len(steps), 3)),
            pltpu.SemaphoreType.DMA((3,)),
        ],
        compiler_params=pltpu.CompilerParams(vmem_limit_bytes=PROJECT_LIMIT),
        cost_estimate=pl.CostEstimate(
            flops=6 * tok * depth * pair * len(steps),
            bytes_accessed=6 * depth * pair * len(steps),
            transcendentals=0,
        ),
        name="project",
    )(tokens, *(pltpu.with_memory_space_constraint(x, pltpu.HBM) for x in (positions.reshape(1, tok), cluster_ids)), *weights)


def pack_kernel(first_ref, second_ref, out_ref):
    tok = (out_ref.shape[0] - META) // 2
    out_ref[:tok, :] = first_ref[:tok, :]
    out_ref[tok : 2 * tok, :] = second_ref[:tok, :]
    first = first_ref[tok : tok + META, :].astype(jnp.float32)
    second = second_ref[tok : tok + META, :].astype(jnp.float32)
    row = lax.broadcasted_iota(jnp.int32, first.shape, 0)
    low = jnp.broadcast_to(second[1:2], first.shape)
    second = jnp.where(row == META // 2, jnp.broadcast_to(second[0:1], first.shape), low)
    out_ref[2 * tok :, :] = jnp.where(row < META // 2, first, second).astype(jnp.bfloat16)


def pack(first, second, tok, flops):
    vmem = pl.BlockSpec(memory_space=pltpu.VMEM)
    wide = first.shape[1]
    return pl.pallas_call(
        pack_kernel,
        out_shape=jax.ShapeDtypeStruct((2 * tok + META, wide), jnp.bfloat16),
        in_specs=[vmem, vmem],
        out_specs=vmem,
        compiler_params=pltpu.CompilerParams(vmem_limit_bytes=PACK_LIMIT),
        cost_estimate=pl.CostEstimate(
            flops=flops, bytes_accessed=8 * tok * wide, transcendentals=0
        ),
        name="pack",
    )(first, second)


def ids_of(ref, item, tok, total):
    pair = ref.shape[1] // 2
    row = 2 * tok + item * (META // 2)
    cid = ref[row : row + 1, :pair].astype(jnp.float32)
    low = ref[row + 1 : row + 2, :pair].astype(jnp.float32)
    high = ref[row : row + 1, pair:].astype(jnp.float32)
    pos = high * float(BASE) + low
    return cid * float(2 * total) + pos, pos


def unpack(refs, tok, total, keys, values, codes):
    pair = keys.shape[1]
    for at, ref in enumerate(refs):
        rows = slice(2 * at * tok, 2 * (at + 1) * tok)
        keys[rows, :] = ref[: 2 * tok, :pair]
        values[rows, :] = ref[: 2 * tok, pair:]
        for item in range(2):
            start = (2 * at + item) * tok
            codes[0:1, start : start + tok] = ids_of(ref, item, tok, total)[0]


def scores_of(q_ref, ids_ref, which, tok, total, keys, codes, column):
    pair = keys.shape[1]
    code, pos = ids_of(ids_ref, which, tok, total)
    column[0:1, :] = code
    column[1:2, :] = pos
    turned = jnp.transpose(column[...])
    gap = turned[:, 0:1] - codes[0:1, :]
    allowed = (gap >= 0.0) & (gap <= turned[:, 1:2])
    bias = jnp.where(allowed, 0.0, -1e30)
    start = q_ref.shape[0] - tok // 2
    query = jnp.concatenate([q_ref[start:, :pair], q_ref[start:, pair:]], axis=0)
    lane = lax.broadcasted_iota(jnp.int32, (tok, pair), 1) < HD
    none = jnp.zeros_like(query)
    both = jnp.concatenate([jnp.where(lane, query, none), jnp.where(lane, none, query)], axis=0)
    scores = lax.dot_general(
        both, keys[...], (((1,), (1,)), ((), ())), preferred_element_type=jnp.float32
    )
    return scores * (HD**-0.5 * LOG2E) + jnp.concatenate([bias, bias], axis=0)


def early_kernel(total, tok, count, *refs):
    q_refs = refs[:SPLIT]
    kv_refs = refs[SPLIT : SPLIT + count]
    expo_ref, stats_ref, values, keys, codes, column = refs[SPLIT + count :]
    unpack(kv_refs, tok, total, keys, values, codes)
    for item in range(SPLIT):
        scores = scores_of(
            q_refs[item], kv_refs[item // 2], item % 2, tok, total, keys, codes, column
        )
        top = jnp.max(scores, axis=1, keepdims=True)
        expo = jnp.exp2(scores - top)
        rows = slice(item * 2 * tok, (item + 1) * 2 * tok)
        expo_ref[rows, :] = expo
        stats_ref[rows, 0:1] = top
        stats_ref[rows, 1:2] = jnp.sum(expo, axis=1, keepdims=True)


def early(total, tok, queries, sources):
    wide = sources[0].shape[1]
    pair = wide // 2
    vmem = pl.BlockSpec(memory_space=pltpu.VMEM)
    count = 2 * tok * len(sources)
    rows = 2 * SPLIT * tok
    return pl.pallas_call(
        functools.partial(early_kernel, total, tok, len(sources)),
        out_shape=(
            jax.ShapeDtypeStruct((rows, count), jnp.float32),
            jax.ShapeDtypeStruct((rows, pair), jnp.float32),
            jax.ShapeDtypeStruct((count, pair), jnp.bfloat16),
        ),
        in_specs=[vmem] * (len(queries) + len(sources)),
        out_specs=(vmem,) * 3,
        scratch_shapes=[
            pltpu.VMEM((count, pair), jnp.bfloat16),
            pltpu.VMEM((8, count), jnp.float32),
            pltpu.VMEM((8, tok), jnp.float32),
        ],
        compiler_params=pltpu.CompilerParams(vmem_limit_bytes=ATTEND_LIMIT),
        cost_estimate=pl.CostEstimate(
            flops=EARLY_FLOPS, bytes_accessed=8 * count * pair, transcendentals=rows * count
        ),
        name="early",
    )(*queries, *sources)


def late_kernel(total, tok, items, count, *refs):
    many = len(items)
    q_refs, ids_refs = refs[:many], refs[many : 2 * many]
    expo_ref, stats_ref, old_values = refs[2 * many : 2 * many + 3]
    kv_refs = refs[2 * many + 3 : 2 * many + 3 + count]
    out_refs = refs[2 * many + 3 + count : 3 * many + 3 + count]
    keys, values, codes, column = refs[3 * many + 3 + count :]
    unpack(kv_refs, tok, total, keys, values, codes)
    pair = keys.shape[1]
    lane = lax.broadcasted_iota(jnp.int32, (tok, pair), 1) < HD
    for at, item in enumerate(items):
        scores = scores_of(q_refs[at], ids_refs[at], item % 2, tok, total, keys, codes, column)
        rows = slice(item * 2 * tok, (item + 1) * 2 * tok)
        old_top = stats_ref[rows, 0:1]
        top = jnp.maximum(jnp.max(scores, axis=1, keepdims=True), old_top)
        expo = jnp.exp2(scores - top)
        factor = jnp.exp2(old_top - top)
        inverse = 1.0 / (jnp.sum(expo, axis=1, keepdims=True) + stats_ref[rows, 1:2] * factor)
        result = jnp.dot(
            (expo_ref[rows, :] * (factor * inverse)).astype(jnp.bfloat16),
            old_values[...],
            preferred_element_type=jnp.float32,
        )
        result += jnp.dot(
            (expo * inverse).astype(jnp.bfloat16), values[...], preferred_element_type=jnp.float32
        )
        out_refs[at][...] = jnp.where(lane, result[:tok], result[tok:]).astype(jnp.bfloat16)


def late(total, tok, items, queries, ids, expo, stats, old_values, sources):
    pair = old_values.shape[1]
    vmem = pl.BlockSpec(memory_space=pltpu.VMEM)
    count = 2 * tok * len(sources)
    return pl.pallas_call(
        functools.partial(late_kernel, total, tok, items, len(sources)),
        out_shape=(jax.ShapeDtypeStruct((tok, pair), jnp.bfloat16),) * len(items),
        in_specs=[vmem] * (2 * len(items) + 3 + len(sources)),
        out_specs=(vmem,) * len(items),
        scratch_shapes=[
            pltpu.VMEM((count, pair), jnp.bfloat16),
            pltpu.VMEM((count, pair), jnp.bfloat16),
            pltpu.VMEM((8, count), jnp.float32),
            pltpu.VMEM((8, tok), jnp.float32),
        ],
        compiler_params=pltpu.CompilerParams(vmem_limit_bytes=ATTEND_LIMIT),
        cost_estimate=pl.CostEstimate(
            flops=LATE_FLOPS,
            bytes_accessed=4 * count * pair,
            transcendentals=2 * len(items) * tok * count,
        ),
        name="late",
    )(*queries, *ids, expo, stats, old_values, *sources)


def mix_kernel(with_sum, *refs):
    piece_refs, (w_ref, *sum_refs, out_ref, rows_buf) = refs[:SPLIT], refs[SPLIT:]
    rows, pair = out_ref.shape[0], piece_refs[0].shape[1]
    chip = lax.axis_index("seq") // PLANE
    mine = pl.ds(pl.multiple_of(lax.axis_index("head") * rows, rows), rows)
    for step in range(SPLIT):
        lanes = pl.ds(pl.multiple_of(jnp.bitwise_xor(chip, step) * pair, pair), pair)
        rows_buf[:, lanes] = piece_refs[step][mine, :]
    total = jnp.dot(rows_buf[...], w_ref[...], preferred_element_type=jnp.float32)
    if with_sum:
        total += sum_refs[0][...]
    out_ref[...] = total.astype(out_ref.dtype)


def mix(pieces, weight, before=None):
    rows = pieces[0].shape[0] // 2
    deep, width = weight.shape
    vmem = pl.BlockSpec(memory_space=pltpu.VMEM)
    sums = [] if before is None else [before]
    dtype = jnp.float32 if before is None else jnp.bfloat16
    return pl.pallas_call(
        functools.partial(mix_kernel, before is not None),
        out_shape=jax.ShapeDtypeStruct((rows, width), dtype),
        in_specs=[vmem] * (SPLIT + 1 + len(sums)),
        out_specs=vmem,
        scratch_shapes=[pltpu.VMEM((rows, deep), jnp.bfloat16)],
        compiler_params=pltpu.CompilerParams(vmem_limit_bytes=PACK_LIMIT),
        cost_estimate=pl.CostEstimate(
            flops=2 * rows * deep * width, bytes_accessed=2 * deep * width, transcendentals=0
        ),
        name="mix",
    )(*pieces, weight, *sums)


def per_device_split(tokens, w_query, w_key, w_value, w_out, cluster_ids, positions):
    tok = tokens.shape[0]
    owners = lax.axis_size("seq")

    def send(array, bits):
        return lax.ppermute(array, "seq", [(i, i ^ bits) for i in range(owners)])

    def swap(array):
        return lax.ppermute(array, "head", [(0, 1), (1, 0)])

    w_other = swap(w_out)
    weights = (w_query, w_key, w_value)
    m1, kv0, q0, m3, m2 = project((1, 0, 3, 2), tokens, positions, cluster_ids, weights)
    r1, r3, r2 = send(m1, PLANE), send(m3, 3 * PLANE), send(m2, 2 * PLANE)
    kv0, w_other = lax.optimization_barrier((kv0, w_other))
    near = pack(kv0, r1, tok, 0)
    nears = [send(near, bits) for bits in (1, 2, 3)]
    far = pack(r2, r3, tok, FAR_FLOPS)
    far, nears[1] = lax.optimization_barrier((far, nears[1]))
    fars = [send(far, bits) for bits in (3, 1, 2)]
    total = owners * tok
    expo, stats, values = early(total, tok, (q0, r1, r2, r3), [near, far, *nears])
    queries, own = (q0, r1, r2, r3), [None] * SPLIT
    for item in (3, 2, 1, 0):
        ids = near if item < 2 else far
        (part,) = late(total, tok, (item,), (queries[item],), (ids,), expo, stats, values, fars)
        part, stats = lax.optimization_barrier((part, stats))
        own[item] = part
    own[3], own[2] = lax.optimization_barrier((own[3], own[2]))
    b3 = send(own[3], 3 * PLANE)
    own = (own[0], send(own[1], PLANE), send(own[2], 2 * PLANE), b3)
    half = mix(own, w_out)
    return mix([swap(item) for item in own], w_other, half)


def attend_rows(query, keys, values, query_pos, key_pos):
    scores = jnp.einsum("qhd,khd->hqk", query, keys, preferred_element_type=jnp.float32) * HD ** (
        -0.5
    )
    allowed = (key_pos[None, None, :] >= 0) & (key_pos[None, None, :] <= query_pos[None, :, None])
    masked = jnp.where(allowed, scores, jnp.float32(-1e30))
    top = jnp.max(masked, axis=-1, keepdims=True)
    expo = jnp.exp(masked - top)
    weights = (expo / jnp.sum(expo, axis=-1, keepdims=True)).astype(jnp.bfloat16)
    return jnp.einsum("hqk,khd->qhd", weights, values, preferred_element_type=jnp.float32).astype(
        jnp.bfloat16
    )


def attend_group(data, pos):
    rows = data.shape[0]
    width = data.shape[1] // 3
    query = data[:, :width].reshape(rows, GROUP_HEADS, HD)
    keys = data[:, width : 2 * width].reshape(rows, GROUP_HEADS, HD)
    values = data[:, 2 * width :].reshape(rows, GROUP_HEADS, HD)
    half = rows // 2
    first = attend_rows(query[:half], keys, values, pos[:half], pos)
    second = attend_rows(query[half:], keys, values, pos[half:], pos)
    result = jnp.concatenate([first, second], axis=0)
    return result.reshape(rows, width)


def owner_side(pieces):
    data, pos = pieces
    outputs = [attend_group(data[:, item], pos[:, item]) for item in range(data.shape[1])]
    result = jnp.stack(outputs, axis=1)
    return lax.all_to_all(result, "seq", split_axis=0, concat_axis=0, tiled=True)


def per_device_owner(tokens, w_query, w_key, w_value, w_out, cluster_ids, positions):
    tok = tokens.shape[0]
    groups_here = cluster_ids.shape[0]
    owners = lax.axis_size("seq")
    half = tok // 2
    fewer = owners // 4
    capacity = (half + owners - 1) // owners + (half + fewer - 1) // fewer
    slots = owners * capacity
    width = w_query.shape[1] // groups_here
    tok_ids = jnp.arange(tok, dtype=jnp.int32)
    earlier = tok_ids[None, :] < tok_ids[:, None]
    same = cluster_ids[:, :, None] == cluster_ids[:, None, :]
    rank = jnp.sum((same & earlier[None]).astype(jnp.int32), axis=2)
    dest = cluster_ids * capacity + rank
    slot_ids = jnp.arange(slots, dtype=jnp.int32)
    matches = slot_ids[None, :, None] == dest[:, None, :]
    onehot = matches.astype(jnp.bfloat16)
    filled = jnp.any(matches, axis=2)
    pos_sum = jnp.sum(jnp.where(matches, positions[None, None, :], 0), axis=2)
    pos_slots = jnp.where(filled, pos_sum, -1).T

    def project_group(index):
        lo = index * width
        parts = [
            jnp.dot(tokens, weight[:, lo : lo + width], preferred_element_type=jnp.float32).astype(
                jnp.bfloat16
            )
            for weight in (w_query, w_key, w_value)
        ]
        return jnp.concatenate(parts, axis=1)

    data = jnp.stack([project_group(index) for index in range(groups_here)], axis=1)
    send = jnp.einsum("gst,tgc->sgc", onehot, data, preferred_element_type=jnp.float32).astype(
        jnp.bfloat16
    )
    back = owner_side(
        (
            lax.all_to_all(send, "seq", split_axis=0, concat_axis=0, tiled=True),
            lax.all_to_all(pos_slots, "seq", split_axis=0, concat_axis=0, tiled=True),
        )
    )
    attended = jnp.einsum("gst,sgc->tgc", onehot, back, preferred_element_type=jnp.float32).astype(
        jnp.bfloat16
    )
    attended = attended.reshape(tok, groups_here * width)
    mixed = lax.psum_scatter(
        jnp.dot(attended, w_out, preferred_element_type=jnp.float32),
        "head",
        scatter_dimension=0,
        tiled=True,
    )
    return mixed.astype(jnp.bfloat16)


def solution(mesh):
    in_specs = (
        P("seq", None),
        P(None, "head"),
        P(None, "head"),
        P(None, "head"),
        P("head", None),
        P("head", "seq"),
        P("seq"),
    )
    out_specs = P(("seq", "head"), None)
    plan = per_device_split if mesh.shape["seq"] == SPLIT * PLANE else per_device_owner
    return jax.shard_map(
        plan, mesh=mesh, in_specs=in_specs, out_specs=out_specs, check_vma=False
    )
```

```python
import functools

import jax
import jax.numpy as jnp
from jax import lax
from jax.experimental import pallas as pl
from jax.experimental.pallas import tpu as pltpu
from jax.sharding import PartitionSpec as P

HD = 64
GROUP_HEADS = 4

SPLIT = 4
PLANE = 4
META = 8
BASE = 128
PROJECT_LIMIT = (53 << 20) + (512 << 10)
PACK_LIMIT = 4 << 20
ATTEND_LIMIT = 16 << 20
FAR_FLOPS = 10**10
EARLY_FLOPS = 8 * 10**9
LATE_FLOPS = 3 * 10**9
LOG2E = 1.4426950408889634


def project_kernel(steps, tok_hbm, pos_hbm, cid_hbm, wq_ref, wk_ref, wv_ref, *rest):
    out_refs = list(rest[:-6])
    rows, pos_ref, cid_ref, wbuf, sems, small_sems = rest[-6:]
    tok, pair = rows.shape[0], wbuf.shape[2] // 3
    chip = lax.axis_index("seq") // PLANE
    small = [
        pltpu.make_async_copy(source, target, small_sems.at[at])
        for at, (source, target) in enumerate(
            ((tok_hbm, rows), (pos_hbm, pos_ref), (cid_hbm, cid_ref))
        )
    ]
    for copy in small:
        copy.start()
    copies = []
    for at, step in enumerate(steps):
        lanes = pl.ds(pl.multiple_of(jnp.bitwise_xor(chip, step) * pair, pair), pair)
        for part, w_ref in enumerate((wq_ref, wk_ref, wv_ref)):
            target = wbuf.at[at, :, pl.ds(part * pair, pair)]
            copy = pltpu.make_async_copy(w_ref.at[:, lanes], target, sems.at[at, part])
            copy.start()
            copies.append(copy)
    for copy in small:
        copy.wait()
    high_digit = jnp.broadcast_to(pos_ref[...] // BASE, (META, tok))
    low_digit = jnp.broadcast_to(pos_ref[...] % BASE, (META, tok))
    first = lax.broadcasted_iota(jnp.int32, (META, tok), 0) == 0
    for at, step in enumerate(steps):
        for part in range(3):
            copies[3 * at + part].wait()
        result = jnp.dot(rows[...], wbuf[at], preferred_element_type=jnp.float32)
        result = result.astype(jnp.bfloat16)
        kv_ref = out_refs.pop(0)
        kv_ref[:tok, :] = result[:, pair:]
        who = jnp.bitwise_xor(chip, step)
        ids = jnp.where(who >= SPLIT // 2, cid_ref[1:2, :], cid_ref[0:1, :])
        left = jnp.where(first, jnp.broadcast_to(ids, (META, tok)), low_digit)
        kv_ref[tok : tok + META, :pair] = left.astype(jnp.float32).astype(jnp.bfloat16)
        kv_ref[tok : tok + META, pair:] = high_digit.astype(jnp.float32).astype(jnp.bfloat16)
        q_ref, base = (kv_ref, tok + META) if step else (out_refs.pop(0), 0)
        q_ref[base : base + tok // 2, :pair] = result[: tok // 2, :pair]
        q_ref[base : base + tok // 2, pair:] = result[tok // 2 :, :pair]


def project(steps, tokens, positions, cluster_ids, weights):
    tok, depth = tokens.shape
    pair = weights[0].shape[1] // SPLIT
    vmem = pl.BlockSpec(memory_space=pltpu.VMEM)
    hbm = pl.BlockSpec(memory_space=pltpu.HBM)
    sizes = []
    for step in steps:
        sizes += [tok + META + tok // 2] if step else [tok + META, tok // 2]
    return pl.pallas_call(
        functools.partial(project_kernel, steps),
        out_shape=tuple(jax.ShapeDtypeStruct((rows, 2 * pair), jnp.bfloat16) for rows in sizes),
        in_specs=[hbm] * 6,
        out_specs=(vmem,) * len(sizes),
        scratch_shapes=[
            pltpu.VMEM((tok, depth), jnp.bfloat16),
            pltpu.VMEM((1, tok), jnp.int32),
            pltpu.VMEM(cluster_ids.shape, jnp.int32),
            pltpu.VMEM((len(steps), depth, 3 * pair), jnp.bfloat16),
            pltpu.SemaphoreType.DMA((len(steps), 3)),
            pltpu.SemaphoreType.DMA((3,)),
        ],
        compiler_params=pltpu.CompilerParams(vmem_limit_bytes=PROJECT_LIMIT),
        cost_estimate=pl.CostEstimate(
            flops=6 * tok * depth * pair * len(steps),
            bytes_accessed=6 * depth * pair * len(steps),
            transcendentals=0,
        ),
        name="project",
    )(tokens, *(pltpu.with_memory_space_constraint(x, pltpu.HBM) for x in (positions.reshape(1, tok), cluster_ids)), *weights)


def pack_kernel(first_ref, second_ref, out_ref):
    tok = (out_ref.shape[0] - META) // 2
    out_ref[:tok, :] = first_ref[:tok, :]
    out_ref[tok : 2 * tok, :] = second_ref[:tok, :]
    first = first_ref[tok : tok + META, :].astype(jnp.float32)
    second = second_ref[tok : tok + META, :].astype(jnp.float32)
    row = lax.broadcasted_iota(jnp.int32, first.shape, 0)
    low = jnp.broadcast_to(second[1:2], first.shape)
    second = jnp.where(row == META // 2, jnp.broadcast_to(second[0:1], first.shape), low)
    out_ref[2 * tok :, :] = jnp.where(row < META // 2, first, second).astype(jnp.bfloat16)


def pack(first, second, tok, flops):
    vmem = pl.BlockSpec(memory_space=pltpu.VMEM)
    wide = first.shape[1]
    return pl.pallas_call(
        pack_kernel,
        out_shape=jax.ShapeDtypeStruct((2 * tok + META, wide), jnp.bfloat16),
        in_specs=[vmem, vmem],
        out_specs=vmem,
        compiler_params=pltpu.CompilerParams(vmem_limit_bytes=PACK_LIMIT),
        cost_estimate=pl.CostEstimate(
            flops=flops, bytes_accessed=8 * tok * wide, transcendentals=0
        ),
        name="pack",
    )(first, second)


def ids_of(ref, item, tok, total):
    pair = ref.shape[1] // 2
    row = 2 * tok + item * (META // 2)
    cid = ref[row : row + 1, :pair].astype(jnp.float32)
    low = ref[row + 1 : row + 2, :pair].astype(jnp.float32)
    high = ref[row : row + 1, pair:].astype(jnp.float32)
    pos = high * float(BASE) + low
    return cid * float(2 * total) + pos, pos


def unpack(refs, tok, total, keys, values, codes):
    pair = keys.shape[1]
    for at, ref in enumerate(refs):
        rows = slice(2 * at * tok, 2 * (at + 1) * tok)
        keys[rows, :] = ref[: 2 * tok, :pair]
        values[rows, :] = ref[: 2 * tok, pair:]
        for item in range(2):
            start = (2 * at + item) * tok
            codes[0:1, start : start + tok] = ids_of(ref, item, tok, total)[0]


def scores_of(q_ref, ids_ref, which, tok, total, keys, codes, column):
    pair = keys.shape[1]
    code, pos = ids_of(ids_ref, which, tok, total)
    column[0:1, :] = code
    column[1:2, :] = pos
    turned = jnp.transpose(column[...])
    gap = turned[:, 0:1] - codes[0:1, :]
    allowed = (gap >= 0.0) & (gap <= turned[:, 1:2])
    bias = jnp.where(allowed, 0.0, -1e30)
    start = q_ref.shape[0] - tok // 2
    query = jnp.concatenate([q_ref[start:, :pair], q_ref[start:, pair:]], axis=0)
    lane = lax.broadcasted_iota(jnp.int32, (tok, pair), 1) < HD
    none = jnp.zeros_like(query)
    both = jnp.concatenate([jnp.where(lane, query, none), jnp.where(lane, none, query)], axis=0)
    scores = lax.dot_general(
        both, keys[...], (((1,), (1,)), ((), ())), preferred_element_type=jnp.float32
    )
    return scores * (HD**-0.5 * LOG2E) + jnp.concatenate([bias, bias], axis=0)


def early_kernel(total, tok, count, *refs):
    q_refs = refs[:SPLIT]
    kv_refs = refs[SPLIT : SPLIT + count]
    expo_ref, stats_ref, values, keys, codes, column = refs[SPLIT + count :]
    unpack(kv_refs, tok, total, keys, values, codes)
    for item in range(SPLIT):
        scores = scores_of(
            q_refs[item], kv_refs[item // 2], item % 2, tok, total, keys, codes, column
        )
        top = jnp.max(scores, axis=1, keepdims=True)
        expo = jnp.exp2(scores - top)
        rows = slice(item * 2 * tok, (item + 1) * 2 * tok)
        expo_ref[rows, :] = expo
        stats_ref[rows, 0:1] = top
        stats_ref[rows, 1:2] = jnp.sum(expo, axis=1, keepdims=True)


def early(total, tok, queries, sources):
    wide = sources[0].shape[1]
    pair = wide // 2
    vmem = pl.BlockSpec(memory_space=pltpu.VMEM)
    count = 2 * tok * len(sources)
    rows = 2 * SPLIT * tok
    return pl.pallas_call(
        functools.partial(early_kernel, total, tok, len(sources)),
        out_shape=(
            jax.ShapeDtypeStruct((rows, count), jnp.float32),
            jax.ShapeDtypeStruct((rows, pair), jnp.float32),
            jax.ShapeDtypeStruct((count, pair), jnp.bfloat16),
        ),
        in_specs=[vmem] * (len(queries) + len(sources)),
        out_specs=(vmem,) * 3,
        scratch_shapes=[
            pltpu.VMEM((count, pair), jnp.bfloat16),
            pltpu.VMEM((8, count), jnp.float32),
            pltpu.VMEM((8, tok), jnp.float32),
        ],
        compiler_params=pltpu.CompilerParams(vmem_limit_bytes=ATTEND_LIMIT),
        cost_estimate=pl.CostEstimate(
            flops=EARLY_FLOPS, bytes_accessed=8 * count * pair, transcendentals=rows * count
        ),
        name="early",
    )(*queries, *sources)


def late_kernel(total, tok, items, count, *refs):
    many = len(items)
    q_refs, ids_refs = refs[:many], refs[many : 2 * many]
    expo_ref, stats_ref, old_values = refs[2 * many : 2 * many + 3]
    kv_refs = refs[2 * many + 3 : 2 * many + 3 + count]
    out_refs = refs[2 * many + 3 + count : 3 * many + 3 + count]
    keys, values, codes, column = refs[3 * many + 3 + count :]
    unpack(kv_refs, tok, total, keys, values, codes)
    pair = keys.shape[1]
    lane = lax.broadcasted_iota(jnp.int32, (tok, pair), 1) < HD
    for at, item in enumerate(items):
        scores = scores_of(q_refs[at], ids_refs[at], item % 2, tok, total, keys, codes, column)
        rows = slice(item * 2 * tok, (item + 1) * 2 * tok)
        old_top = stats_ref[rows, 0:1]
        top = jnp.maximum(jnp.max(scores, axis=1, keepdims=True), old_top)
        expo = jnp.exp2(scores - top)
        factor = jnp.exp2(old_top - top)
        inverse = 1.0 / (jnp.sum(expo, axis=1, keepdims=True) + stats_ref[rows, 1:2] * factor)
        result = jnp.dot(
            (expo_ref[rows, :] * (factor * inverse)).astype(jnp.bfloat16),
            old_values[...],
            preferred_element_type=jnp.float32,
        )
        result += jnp.dot(
            (expo * inverse).astype(jnp.bfloat16), values[...], preferred_element_type=jnp.float32
        )
        out_refs[at][...] = jnp.where(lane, result[:tok], result[tok:]).astype(jnp.bfloat16)


def late(total, tok, items, queries, ids, expo, stats, old_values, sources):
    pair = old_values.shape[1]
    vmem = pl.BlockSpec(memory_space=pltpu.VMEM)
    count = 2 * tok * len(sources)
    return pl.pallas_call(
        functools.partial(late_kernel, total, tok, items, len(sources)),
        out_shape=(jax.ShapeDtypeStruct((tok, pair), jnp.bfloat16),) * len(items),
        in_specs=[vmem] * (2 * len(items) + 3 + len(sources)),
        out_specs=(vmem,) * len(items),
        scratch_shapes=[
            pltpu.VMEM((count, pair), jnp.bfloat16),
            pltpu.VMEM((count, pair), jnp.bfloat16),
            pltpu.VMEM((8, count), jnp.float32),
            pltpu.VMEM((8, tok), jnp.float32),
        ],
        compiler_params=pltpu.CompilerParams(vmem_limit_bytes=ATTEND_LIMIT),
        cost_estimate=pl.CostEstimate(
            flops=LATE_FLOPS,
            bytes_accessed=4 * count * pair,
            transcendentals=2 * len(items) * tok * count,
        ),
        name="late",
    )(*queries, *ids, expo, stats, old_values, *sources)


def mix_kernel(with_sum, *refs):
    piece_refs, (w_ref, *sum_refs, out_ref, rows_buf) = refs[:SPLIT], refs[SPLIT:]
    rows, pair = out_ref.shape[0], piece_refs[0].shape[1]
    chip = lax.axis_index("seq") // PLANE
    mine = pl.ds(pl.multiple_of(lax.axis_index("head") * rows, rows), rows)
    for step in range(SPLIT):
        lanes = pl.ds(pl.multiple_of(jnp.bitwise_xor(chip, step) * pair, pair), pair)
        rows_buf[:, lanes] = piece_refs[step][mine, :]
    total = jnp.dot(rows_buf[...], w_ref[...], preferred_element_type=jnp.float32)
    if with_sum:
        total += sum_refs[0][...]
    out_ref[...] = total.astype(out_ref.dtype)


def mix(pieces, weight, before=None):
    rows = pieces[0].shape[0] // 2
    deep, width = weight.shape
    vmem = pl.BlockSpec(memory_space=pltpu.VMEM)
    sums = [] if before is None else [before]
    dtype = jnp.float32 if before is None else jnp.bfloat16
    return pl.pallas_call(
        functools.partial(mix_kernel, before is not None),
        out_shape=jax.ShapeDtypeStruct((rows, width), dtype),
        in_specs=[vmem] * (SPLIT + 1 + len(sums)),
        out_specs=vmem,
        scratch_shapes=[pltpu.VMEM((rows, deep), jnp.bfloat16)],
        compiler_params=pltpu.CompilerParams(vmem_limit_bytes=PACK_LIMIT),
        cost_estimate=pl.CostEstimate(
            flops=2 * rows * deep * width, bytes_accessed=2 * deep * width, transcendentals=0
        ),
        name="mix",
    )(*pieces, weight, *sums)


def per_device_split(tokens, w_query, w_key, w_value, w_out, cluster_ids, positions):
    tok = tokens.shape[0]
    owners = lax.axis_size("seq")

    def send(array, bits):
        return lax.ppermute(array, "seq", [(i, i ^ bits) for i in range(owners)])

    def swap(array):
        return lax.ppermute(array, "head", [(0, 1), (1, 0)])

    weights = (w_query, w_key, w_value)
    m1, kv0, q0, m3, m2 = project((1, 0, 3, 2), tokens, positions, cluster_ids, weights)
    m1, w_late = lax.optimization_barrier((m1, w_out))
    w_other = swap(w_late)
    r1, r3, r2 = send(m1, PLANE), send(m3, 3 * PLANE), send(m2, 2 * PLANE)
    kv0, w_other = lax.optimization_barrier((kv0, w_other))
    near = pack(kv0, r1, tok, 0)
    nears = [send(near, bits) for bits in (1, 2, 3)]
    far = pack(r2, r3, tok, FAR_FLOPS)
    far, nears[1] = lax.optimization_barrier((far, nears[1]))
    fars = [send(far, bits) for bits in (3, 1, 2)]
    total = owners * tok
    expo, stats, values = early(total, tok, (q0, r1, r2, r3), [near, far, *nears])
    queries, own = (q0, r1, r2, r3), [None] * SPLIT
    for item in (3, 2, 1, 0):
        ids = near if item < 2 else far
        (part,) = late(total, tok, (item,), (queries[item],), (ids,), expo, stats, values, fars)
        part, stats = lax.optimization_barrier((part, stats))
        own[item] = part
    own[3], own[2] = lax.optimization_barrier((own[3], own[2]))
    b3 = send(own[3], 3 * PLANE)
    own = (own[0], send(own[1], PLANE), send(own[2], 2 * PLANE), b3)
    half = mix(own, w_out)
    return mix([swap(item) for item in own], w_other, half)


def attend_rows(query, keys, values, query_pos, key_pos):
    scores = jnp.einsum("qhd,khd->hqk", query, keys, preferred_element_type=jnp.float32) * HD ** (
        -0.5
    )
    allowed = (key_pos[None, None, :] >= 0) & (key_pos[None, None, :] <= query_pos[None, :, None])
    masked = jnp.where(allowed, scores, jnp.float32(-1e30))
    top = jnp.max(masked, axis=-1, keepdims=True)
    expo = jnp.exp(masked - top)
    weights = (expo / jnp.sum(expo, axis=-1, keepdims=True)).astype(jnp.bfloat16)
    return jnp.einsum("hqk,khd->qhd", weights, values, preferred_element_type=jnp.float32).astype(
        jnp.bfloat16
    )


def attend_group(data, pos):
    rows = data.shape[0]
    width = data.shape[1] // 3
    query = data[:, :width].reshape(rows, GROUP_HEADS, HD)
    keys = data[:, width : 2 * width].reshape(rows, GROUP_HEADS, HD)
    values = data[:, 2 * width :].reshape(rows, GROUP_HEADS, HD)
    half = rows // 2
    first = attend_rows(query[:half], keys, values, pos[:half], pos)
    second = attend_rows(query[half:], keys, values, pos[half:], pos)
    result = jnp.concatenate([first, second], axis=0)
    return result.reshape(rows, width)


def owner_side(pieces):
    data, pos = pieces
    outputs = [attend_group(data[:, item], pos[:, item]) for item in range(data.shape[1])]
    result = jnp.stack(outputs, axis=1)
    return lax.all_to_all(result, "seq", split_axis=0, concat_axis=0, tiled=True)


def per_device_owner(tokens, w_query, w_key, w_value, w_out, cluster_ids, positions):
    tok = tokens.shape[0]
    groups_here = cluster_ids.shape[0]
    owners = lax.axis_size("seq")
    half = tok // 2
    fewer = owners // 4
    capacity = (half + owners - 1) // owners + (half + fewer - 1) // fewer
    slots = owners * capacity
    width = w_query.shape[1] // groups_here
    tok_ids = jnp.arange(tok, dtype=jnp.int32)
    earlier = tok_ids[None, :] < tok_ids[:, None]
    same = cluster_ids[:, :, None] == cluster_ids[:, None, :]
    rank = jnp.sum((same & earlier[None]).astype(jnp.int32), axis=2)
    dest = cluster_ids * capacity + rank
    slot_ids = jnp.arange(slots, dtype=jnp.int32)
    matches = slot_ids[None, :, None] == dest[:, None, :]
    onehot = matches.astype(jnp.bfloat16)
    filled = jnp.any(matches, axis=2)
    pos_sum = jnp.sum(jnp.where(matches, positions[None, None, :], 0), axis=2)
    pos_slots = jnp.where(filled, pos_sum, -1).T

    def project_group(index):
        lo = index * width
        parts = [
            jnp.dot(tokens, weight[:, lo : lo + width], preferred_element_type=jnp.float32).astype(
                jnp.bfloat16
            )
            for weight in (w_query, w_key, w_value)
        ]
        return jnp.concatenate(parts, axis=1)

    data = jnp.stack([project_group(index) for index in range(groups_here)], axis=1)
    send = jnp.einsum("gst,tgc->sgc", onehot, data, preferred_element_type=jnp.float32).astype(
        jnp.bfloat16
    )
    back = owner_side(
        (
            lax.all_to_all(send, "seq", split_axis=0, concat_axis=0, tiled=True),
            lax.all_to_all(pos_slots, "seq", split_axis=0, concat_axis=0, tiled=True),
        )
    )
    attended = jnp.einsum("gst,sgc->tgc", onehot, back, preferred_element_type=jnp.float32).astype(
        jnp.bfloat16
    )
    attended = attended.reshape(tok, groups_here * width)
    mixed = lax.psum_scatter(
        jnp.dot(attended, w_out, preferred_element_type=jnp.float32),
        "head",
        scatter_dimension=0,
        tiled=True,
    )
    return mixed.astype(jnp.bfloat16)


def solution(mesh):
    in_specs = (
        P("seq", None),
        P(None, "head"),
        P(None, "head"),
        P(None, "head"),
        P("head", None),
        P("head", "seq"),
        P("seq"),
    )
    out_specs = P(("seq", "head"), None)
    plan = per_device_split if mesh.shape["seq"] == SPLIT * PLANE else per_device_owner
    return jax.shard_map(
        plan, mesh=mesh, in_specs=in_specs, out_specs=out_specs, check_vma=False
    )
```
